128 devices in a mesh: seq: 4 (over y_lo, core), tensor: 32 (over z, x, y_hi).
Axes of the slice: x: 4, y: 4 (y_hi: 2, y_lo: 2; y = y_hi * 2 + y_lo), z: 4, core: 2. Of those that a mesh axis runs over, the one named last changes fastest.
Arguments:
- tokens: bfloat16 [1024, 8192], P(('seq', 'tensor')), may hold values from -6 to 6
- gate_blocks: bfloat16 [32, 336, 128, 128], P('tensor', 'seq'), may hold values from -0.09375 to 0.09375
- gate_slots: int32 [32, 336], P('tensor', 'seq'), may hold values from 0 to 447, as said below
- up_blocks: bfloat16 [32, 336, 128, 128], P('tensor', 'seq'), may hold values from -0.09375 to 0.09375
- up_slots: int32 [32, 336], P('tensor', 'seq'), may hold values from 0 to 447, as said below
- down_blocks: bfloat16 [32, 336, 128, 128], P('tensor', 'seq'), may hold values from -0.046875 to 0.046875
- down_slots: int32 [32, 336], P('tensor', 'seq'), may hold values from 0 to 447, as said below
- block_counts: int32 [32, 3], P('tensor'), may hold values from 84 to 336, as said below
Outputs:
- layer_out: bfloat16 [1024, 8192], P(('seq', 'tensor'))
The draws below stay inside these ranges and needn't reach their ends.
Inputs may be any that keep to these rules, and one draw needn't show every extreme that they name: `gate_slots`: within each shard the 336 entries are distinct; only the first block_counts[s, 0] entries of shard s are used. `up_slots`: within each shard the 336 entries are distinct; only the first block_counts[s, 1] entries of shard s are used. `down_slots`: within each shard the 336 entries are distinct; only the first block_counts[s, 2] entries of shard s are used. `block_counts`: for each of the three matrices some shard has exactly 336 live slots in every draw.
All inputs are finite; a program needn't handle non-finite values.
Results may differ from the reference program's by a relative error of at most 0.0049.
Values may be sent and summed in bfloat16 or wider, within the bound.
A program may use at most 192 MiB of HBM per device.

```python
import jax
import jax.numpy as jnp
from jax import lax

D = 8192
FF = 28672
BLK = 128
TOKENS = 1024
SHARDS = 32
ROW_BLOCKS = 64
SHARD_BLOCKS = 7
SLOTS = 336


def shard_slots(key):
    shard_keys = jax.random.split(key, SHARDS)

    def permuted(one_key):
        return jax.random.permutation(one_key, ROW_BLOCKS * SHARD_BLOCKS)[:SLOTS]
    return jax.vmap(permuted)(shard_keys).astype(jnp.int32)


def draw_gate_slots(key, part):
    return shard_slots(jax.random.fold_in(key, 11))


def draw_up_slots(key, part):
    return shard_slots(jax.random.fold_in(key, 12))


def draw_down_slots(key, part):
    return shard_slots(jax.random.fold_in(key, 13))


def draw_block_counts(key, part):
    count_key = jax.random.fold_in(key, 21)
    drawn_counts = jax.random.randint(jax.random.fold_in(count_key, 1), (SHARDS, 3), SLOTS // 4, SLOTS + 1, dtype=jnp.int32)
    fullest = jax.random.randint(jax.random.fold_in(count_key, 2), (3,), 0, SHARDS, dtype=jnp.int32)
    is_top = jnp.arange(SHARDS, dtype=jnp.int32)[:, None] == fullest[None, :]
    return jnp.where(is_top, SLOTS, drawn_counts).astype(jnp.int32)


def block_levels(key, dims, cuts, low, high):
    factor_of = 1.0
    for position, blocks in cuts:
        heights = jax.random.uniform(jax.random.fold_in(jax.random.fold_in(key, 6), position), (blocks,), jnp.float32, low / len(cuts), high / len(cuts))
        factor_of = factor_of * jnp.repeat(jnp.exp(heights), dims[position] // blocks).reshape((-1,) + (1,) * (len(dims) - 1 - position))
    return factor_of


def scatter_about(own_key, extent, spread, reach, shards=(), held_as=jnp.bfloat16):
    factor_of = block_levels(own_key, extent, shards, -0.22, 0.18) if shards else 1.0
    result = jax.random.normal(own_key, extent, jnp.float32) * spread * factor_of
    return jnp.minimum(jnp.maximum(result, -reach), reach).astype(held_as)


def setup_inputs(seed: int = 0) -> dict:
    arg_keys = jax.random.split(jax.random.key(seed), 9)
    return {
        "tokens": scatter_about(arg_keys[0], (TOKENS, D), 1.0, 6.0, ((0, 128),)),
        "gate_blocks": scatter_about(arg_keys[1], (SHARDS, SLOTS, BLK, BLK), (D // 2) ** -0.5, 0.09375, ((0, 32), (1, 4))),
        "gate_slots": draw_gate_slots(jax.random.fold_in(arg_keys[8], 71), 0),
        "up_blocks": scatter_about(arg_keys[3], (SHARDS, SLOTS, BLK, BLK), (D // 2) ** -0.5, 0.09375, ((0, 32), (1, 4))),
        "up_slots": draw_up_slots(jax.random.fold_in(arg_keys[8], 71), 0),
        "down_blocks": scatter_about(arg_keys[5], (SHARDS, SLOTS, BLK, BLK), (FF // 2) ** -0.5, 0.046875, ((0, 32), (1, 4))),
        "down_slots": draw_down_slots(jax.random.fold_in(arg_keys[8], 71), 0),
        "block_counts": draw_block_counts(jax.random.fold_in(arg_keys[8], 71), 0),
    }


def densify(values, slot_ids, live_mask, outer_count, inner_count):
    block_size = values.shape[-1]
    one_hot = jnp.where(live_mask[:, None] & (slot_ids[:, None] == jnp.arange(outer_count * inner_count, dtype=jnp.int32)[None, :]), 1.0, 0.0).astype(jnp.bfloat16)
    flattened = values.reshape(values.shape[0], block_size * block_size)
    placed = jnp.dot(one_hot.T, flattened, preferred_element_type=jnp.float32).astype(jnp.bfloat16)
    placed = placed.reshape(outer_count, inner_count, block_size, block_size)
    return placed.transpose(0, 2, 1, 3).reshape(outer_count * block_size, inner_count * block_size)


def reference(tokens, gate_blocks, gate_slots, up_blocks, up_slots, down_blocks, down_slots, block_counts):
    positions = jnp.arange(SLOTS, dtype=jnp.int32)

    def per_shard(running, inputs):
        gate_values, gate_ids, up_values, up_ids, down_values, down_ids, counts = inputs
        gate_weight = densify(gate_values, gate_ids, positions < counts[0], ROW_BLOCKS, SHARD_BLOCKS)
        up_weight = densify(up_values, up_ids, positions < counts[1], ROW_BLOCKS, SHARD_BLOCKS)
        down_weight = densify(down_values, down_ids, positions < counts[2], SHARD_BLOCKS, ROW_BLOCKS)
        gate_sum = jnp.dot(tokens, gate_weight, preferred_element_type=jnp.float32)
        up_sum = jnp.dot(tokens, up_weight, preferred_element_type=jnp.float32)
        hidden = (jax.nn.silu(gate_sum) * up_sum).astype(jnp.bfloat16)
        return running + jnp.dot(hidden, down_weight, preferred_element_type=jnp.float32), None

    running = jnp.zeros((TOKENS, D), jnp.float32)
    running, ignored = lax.scan(per_shard, running, (gate_blocks, gate_slots, up_blocks, up_slots, down_blocks, down_slots, block_counts))
    return running.astype(jnp.bfloat16)
```

```python
import jax
import jax.numpy as jnp
from jax import lax
from jax.experimental import pallas as pl
from jax.experimental.pallas import tpu as pltpu
from jax.sharding import PartitionSpec as P

MESH = pl.DeviceIdType.MESH
BF16, F32 = jnp.bfloat16, jnp.float32
BLK = 128
TILE = 256
COLS = 7
OWN = 84
NONE = 2 * OWN
TILES = (11, 11, 10)
FIRST = (0, 11, 22)
AXES = (("y", "x", "z"), ("x", "z", "y"), ("z", "y", "x"))
GATHER_CUTS = ((0, 7, 11), (0, 7, 11), (0, 6, 10))
SCATTER_CUTS = ((0, 7, 11), (0, 7, 11), (0, 6, 10))
CHUNKS = 2


def group_index(part, z, x, y):
    at = {"z": z, "x": x, "y": y}
    d1, d2, d3 = AXES[part]
    return (at[d3] * 4 + at[d2]) * 4 + at[d1]


def kernel(
    tok, gate_in, gate_slots, up_in, up_slots, down_in, down_slots, counts, out,
    gate_w, up_w, down_w, first, xs, acc, esend, erecv, hid, r1, s2, r2, s3, r3, tab_v, tab_o, tab,
    w_sem, w_send, w_recv, t_send, t_recv, t_sem, a1s, a1r, a2s, a2r, a3s, a3r, es, er, hs, hr,
    b1s, b1r, b2s, b2r, b3s, b3r,
):
    s, t = lax.axis_index("seq"), lax.axis_index("tensor")
    yl, core = lax.div(s, 2), lax.rem(s, 2)
    z, x, yh = lax.div(t, 8), lax.rem(lax.div(t, 2), 4), lax.rem(t, 2)
    here = {"z": z, "x": x, "y": yh * 2 + yl, "core": core}

    def device(**moved):
        c = {**here, **moved}
        return (lax.rem(c["y"], 2) * 2 + c["core"], c["z"] * 8 + c["x"] * 2 + lax.div(c["y"], 2))

    def along(axis, off):
        return device(**{axis: lax.rem(here[axis] + off, 4)})

    mate = device(core=1 - core)
    pair = device(y=yh * 2 + (1 - yl))

    def remote(src, dst, send, recv, dev):
        return pltpu.make_async_remote_copy(
            src_ref=src, dst_ref=dst, send_sem=send, recv_sem=recv, device_id=dev, device_id_type=MESH
        )

    barrier = pltpu.get_barrier_semaphore()
    for dev in [mate] + [along(a, o) for a in "xyz" for o in (1, 2, 3)]:
        pl.semaphore_signal(barrier, inc=1, device_id=dev, device_id_type=MESH)
    pl.semaphore_wait(barrier, 10)

    gather1 = []
    for p in range(3):
        d1 = AXES[p][0]
        cols = pl.ds(FIRST[p] * TILE, TILES[p] * TILE)
        for o in (1, 2, 3):
            c = remote(tok.at[:, cols], first[p].at[here[d1]], a1s.at[p, o - 1], a1r.at[p, o - 1], along(d1, o))
            c.start()
            gather1.append(c)
    weights = ((gate_in, gate_w), (up_in, up_w), (down_in, down_w))
    local, swap = [], []
    for m, (src, dst) in enumerate(weights):
        local.append(pltpu.make_async_copy(src.at[0], dst.at[pl.ds(0, OWN)], w_sem.at[m]))
        swap.append(remote(src.at[0], dst.at[pl.ds(OWN, OWN)], w_send.at[m], w_recv.at[m], mate))
        local[m].start()
        swap[m].start()
        dst[NONE] = jnp.zeros((BLK, BLK), BF16)

    places = lax.broadcasted_iota(jnp.int32, (8, 128), 0) * 128 + lax.broadcasted_iota(jnp.int32, (8, 128), 1)
    for m, slots in enumerate((gate_slots, up_slots, down_slots)):
        live = counts[0, m] - s * OWN

        def enter(j, table, m=m, slots=slots, live=live):
            i = slots[0, j]
            if m < 2:
                place = lax.rem(i, COLS) * 128 + lax.div(i, COLS)
            else:
                place = lax.div(i, 64) * 128 + lax.rem(i, 64)
            return jnp.where((places == place) & (j < live), j, table)

        tab_v[m] = lax.fori_loop(0, OWN, enter, jnp.full((8, 128), NONE, jnp.int32))
    swap_tab = remote(tab_v, tab_o, t_send.at[0], t_recv.at[0], mate)
    swap_tab.start()

    for p in range(3):
        first[p][here[AXES[p][0]]] = tok[:, FIRST[p] * TILE : (FIRST[p] + TILES[p]) * TILE]

    gather2, gather3 = {}, {}
    for p in range(3):
        d1, d2, d3 = AXES[p]
        for o in range(3):
            gather1[p * 3 + o].wait_recv()

        def regroup(n, _, p=p, d2=d2, d3=d3):
            cols = pl.ds(pl.multiple_of(n * TILE, TILE), TILE)
            rows = [first[p][q, :, cols].astype(F32) for q in range(4)]
            xs[p][n, here[d3], here[d2]] = jnp.concatenate(rows, 0).astype(BF16)
            return 0

        lax.fori_loop(0, TILES[p], regroup, 0)
        for h in range(CHUNKS):
            a, b = GATHER_CUTS[p][h : h + 2]
            part = xs[p].at[pl.ds(a, b - a), here[d3], here[d2]]
            for o in (1, 2, 3):
                c = remote(part, part, a2s.at[h, p, o - 1], a2r.at[h, p, o - 1], along(d2, o))
                c.start()
                gather2[h, p, o] = c
    for h in range(CHUNKS):
        for p in range(3):
            d3 = AXES[p][2]
            a, b = GATHER_CUTS[p][h : h + 2]
            part = xs[p].at[pl.ds(a, b - a), here[d3]]
            for o in (1, 2, 3):
                gather2[h, p, o].wait_recv()
            for o in (1, 2, 3):
                c = remote(part, part, a3s.at[h, p, o - 1], a3r.at[h, p, o - 1], along(d3, o))
                c.start()
                gather3[h, p, o] = c

    swap_tab.wait()
    tab_v[...] = jnp.minimum(tab_v[...], tab_o[...] + OWN)
    to_scalar = pltpu.make_async_copy(tab_v, tab, t_sem.at[0])
    to_scalar.start()
    to_scalar.wait()
    for m in range(3):
        local[m].wait()
        swap[m].wait()

    def project(p, h, j):
        a, b = GATHER_CUTS[p][h : h + 2]
        left = jnp.concatenate([xs[p][n].reshape(512, TILE) for n in range(a, b)], 1)
        rows = []
        for r in range(2 * (FIRST[p] + a), 2 * (FIRST[p] + b)):
            rows.append(jnp.concatenate([gate_w[tab[0, j, r]], up_w[tab[1, j, r]]], 1))
        return jnp.dot(left, jnp.concatenate(rows, 0), preferred_element_type=F32).reshape(64, 8, TILE)

    def sums(j, zz, xx):
        rows = []
        for yy in range(4):
            v = acc[j, 0, group_index(0, zz, xx, yy)]
            v = v + acc[j, 1, group_index(1, zz, xx, yy)]
            rows.append(v + acc[j, 2, group_index(2, zz, xx, yy)])
        return jnp.concatenate(rows, 0)

    for p in range(3):
        for o in (1, 2, 3):
            gather3[0, p, o].wait_recv()

    def project0(j, _):
        for p in range(3):
            acc[j, p] = project(p, 0, j)
        return 0

    lax.fori_loop(0, COLS, project0, 0)
    for p in range(3):
        for o in (1, 2, 3):
            gather3[1, p, o].wait_recv()

    def exchange(j):
        return remote(esend.at[j], erecv.at[j], es.at[j], er.at[j], pair)

    def project1(j, _):
        for p in range(3):
            acc[j, p] = acc[j, p] + project(p, 1, j)

        def fill(i, _):
            zz = lax.div(i, 4)
            esend[j, i] = sums(j, (1 - yl) * 2 + zz, lax.rem(i, 4)).astype(BF16)
            return 0

        lax.fori_loop(0, 8, fill, 0)
        exchange(j).start()
        return 0

    lax.fori_loop(0, COLS, project1, 0)

    def give(j):
        mine = hid.at[0, j, pl.ds(yl * 8, 8)]
        return remote(mine, mine, hs.at[j], hr.at[j], pair)

    def finish(j, _):
        exchange(j).wait_recv()

        def rows(i, _):
            zz = lax.div(i, 4)
            v = sums(j, yl * 2 + zz, lax.rem(i, 4)) + erecv[j, i].astype(F32)
            g, u = v[:, :BLK], v[:, BLK:]
            hid[0, j, yl * 8 + i] = (g / (1.0 + jnp.exp(-g)) * u).astype(BF16)
            return 0

        lax.fori_loop(0, 8, rows, 0)
        give(j).start()
        return 0

    lax.fori_loop(0, COLS, finish, 0)

    def reorder(j, _):
        give(j).wait_recv()
        groups = hid[0, j].astype(F32).reshape(512, BLK)
        for p in (1, 2):
            order = [None] * 64
            for zz in range(4):
                for xx in range(4):
                    for yy in range(4):
                        g = (zz * 4 + xx) * 4 + yy
                        order[group_index(p, zz, xx, yy)] = groups[g * 8 : g * 8 + 8]
            hid[p, j] = jnp.concatenate(order, 0).reshape(16, 32, BLK).astype(BF16)
        return 0

    lax.fori_loop(0, COLS, reorder, 0)
    for c in gather1 + list(gather2.values()) + list(gather3.values()):
        c.wait_send()

    scatter1 = {}
    for h in range(CHUNKS):
        for p in range(3):
            d3 = AXES[p][2]
            a, b = SCATTER_CUTS[p][h : h + 2]

            def down(n, _, p=p):
                left = jnp.concatenate([hid[p, j].reshape(512, BLK) for j in range(COLS)], 1)
                col = 2 * (FIRST[p] + n)
                rows = []
                for j in range(COLS):
                    rows.append(jnp.concatenate([down_w[tab[2, j, col]], down_w[tab[2, j, col + 1]]], 1))
                v = jnp.dot(left, jnp.concatenate(rows, 0), preferred_element_type=F32)
                xs[p][n] = v.astype(BF16).reshape(4, 4, 32, TILE)
                return 0

            lax.fori_loop(a, b, down, 0)
            for o in (1, 2, 3):
                src = xs[p].at[pl.ds(a, b - a), lax.rem(here[d3] + o, 4)]
                c = remote(
                    src, r1[p].at[o - 1, pl.ds(a, b - a)], b1s.at[h, p, o - 1], b1r.at[h, p, o - 1], along(d3, o)
                )
                c.start()
                scatter1[h, p, o] = c
    scatter2 = {}
    for h in range(CHUNKS):
        for p in range(3):
            d2, d3 = AXES[p][1:]
            a, b = SCATTER_CUTS[p][h : h + 2]
            for o in (1, 2, 3):
                scatter1[h, p, o].wait_recv()

            def add1(n, _, p=p, d3=d3):
                v = xs[p][n, here[d3]].astype(F32)
                for o in range(3):
                    v = v + r1[p][o, n].astype(F32)
                s2[p][n] = v.astype(BF16)
                return 0

            lax.fori_loop(a, b, add1, 0)
            for o in (1, 2, 3):
                src = s2[p].at[pl.ds(a, b - a), lax.rem(here[d2] + o, 4)]
                c = remote(
                    src, r2[p].at[o - 1, pl.ds(a, b - a)], b2s.at[h, p, o - 1], b2r.at[h, p, o - 1], along(d2, o)
                )
                c.start()
                scatter2[h, p, o] = c
    scatter3 = {}
    for h in range(CHUNKS):
        for p in range(3):
            d1, d2 = AXES[p][:2]
            a, b = SCATTER_CUTS[p][h : h + 2]
            for o in (1, 2, 3):
                scatter2[h, p, o].wait_recv()

            def add2(n, _, p=p, d2=d2):
                v = s2[p][n, here[d2]].astype(F32)
                for o in range(3):
                    v = v + r2[p][o, n].astype(F32)
                s3[p][n] = v.reshape(4, 8, TILE)
                return 0

            lax.fori_loop(a, b, add2, 0)
            for o in (1, 2, 3):
                src = s3[p].at[pl.ds(a, b - a), lax.rem(here[d1] + o, 4)]
                c = remote(
                    src, r3[p].at[o - 1, pl.ds(a, b - a)], b3s.at[h, p, o - 1], b3r.at[h, p, o - 1], along(d1, o)
                )
                c.start()
                scatter3[h, p, o] = c
    for h in range(CHUNKS):
        for p in range(3):
            d1 = AXES[p][0]
            a, b = SCATTER_CUTS[p][h : h + 2]
            for o in (1, 2, 3):
                scatter3[h, p, o].wait_recv()

            def add3(n, _, p=p, d1=d1):
                v = s3[p][n, here[d1]] + r3[p][0, n] + r3[p][1, n] + r3[p][2, n]
                out[:, pl.ds(pl.multiple_of((FIRST[p] + n) * TILE, TILE), TILE)] = v.astype(BF16)
                return 0

            lax.fori_loop(a, b, add3, 0)

    def sent(j, _):
        exchange(j).wait_send()
        give(j).wait_send()
        return 0

    lax.fori_loop(0, COLS, sent, 0)
    for c in list(scatter1.values()) + list(scatter2.values()) + list(scatter3.values()):
        c.wait_send()


def on_device(tokens, gate_blocks, gate_slots, up_blocks, up_slots, down_blocks, down_slots, block_counts):
    vmem = pl.BlockSpec(memory_space=pltpu.VMEM)
    smem = pl.BlockSpec(memory_space=pltpu.SMEM)
    hbm = pl.BlockSpec(memory_space=pl.ANY)
    dma = pltpu.SemaphoreType.DMA

    def parts(shape, dtype):
        return [pltpu.VMEM(shape(n), dtype) for n in TILES]

    weights = pltpu.VMEM((NONE + 1, BLK, BLK), BF16)
    stage = dma((CHUNKS, 3, 3))
    return pl.pallas_call(
        kernel,
        name="layer",
        out_shape=jax.ShapeDtypeStruct(tokens.shape, BF16),
        in_specs=[vmem, hbm, smem, hbm, smem, hbm, smem, smem],
        out_specs=vmem,
        scratch_shapes=[
            weights,
            weights,
            weights,
            parts(lambda n: (4, 8, n * TILE), BF16),
            parts(lambda n: (n, 4, 4, 32, TILE), BF16),
            pltpu.VMEM((COLS, 3, 64, 8, TILE), F32),
            pltpu.VMEM((COLS, 8, 32, TILE), BF16),
            pltpu.VMEM((COLS, 8, 32, TILE), BF16),
            pltpu.VMEM((3, COLS, 16, 32, BLK), BF16),
            parts(lambda n: (3, n, 4, 32, TILE), BF16),
            parts(lambda n: (n, 4, 32, TILE), BF16),
            parts(lambda n: (3, n, 32, TILE), BF16),
            parts(lambda n: (n, 4, 8, TILE), F32),
            parts(lambda n: (3, n, 8, TILE), F32),
            pltpu.VMEM((3, 8, 128), jnp.int32),
            pltpu.VMEM((3, 8, 128), jnp.int32),
            pltpu.SMEM((3, 8, 128), jnp.int32),
            dma((3,)),
            dma((3,)),
            dma((3,)),
            dma((1,)),
            dma((1,)),
            dma((1,)),
            dma((3, 3)),
            dma((3, 3)),
            stage,
            stage,
            stage,
            stage,
            dma((COLS,)),
            dma((COLS,)),
            dma((COLS,)),
            dma((COLS,)),
            stage,
            stage,
            stage,
            stage,
            stage,
            stage,
        ],
        compiler_params=pltpu.CompilerParams(
            collective_id=0, has_side_effects=True, vmem_limit_bytes=60 * 2**20
        ),
    )(tokens, gate_blocks, gate_slots, up_blocks, up_slots, down_blocks, down_slots, block_counts)


def solution(mesh):
    return jax.shard_map(
        on_device,
        mesh=mesh,
        in_specs=(
            P(("seq", "tensor"), None),
            P("tensor", "seq", None, None),
            P("tensor", "seq"),
            P("tensor", "seq", None, None),
            P("tensor", "seq"),
            P("tensor", "seq", None, None),
            P("tensor", "seq"),
            P("tensor", None),
        ),
        out_specs=P(("seq", "tensor"), None),
        check_vma=False,
    )
```

```python
import jax
import jax.numpy as jnp
from jax import lax
from jax.experimental import pallas as pl
from jax.experimental.pallas import tpu as pltpu
from jax.sharding import PartitionSpec as P

MESH = pl.DeviceIdType.MESH
BF16, F32 = jnp.bfloat16, jnp.float32
BLK = 128
TILE = 256
COLS = 7
OWN = 84
NONE = 2 * OWN
TILES = (12, 8, 12)
FIRST = (0, TILES[0], TILES[0] + TILES[1])
AXES = (("y", "x", "z"), ("x", "z", "y"), ("z", "y", "x"))
PARTS = range(3)
HALVES = 2
CHUNKS = 2
CUTS = tuple((0, n // 2, n) for n in TILES)


def swap4(a, b):
    low = lax.broadcasted_iota(jnp.int32, a.shape, 0) < 4
    return jnp.where(low, a, pltpu.roll(b, 4, 0)), jnp.where(low, pltpu.roll(a, 4, 0), b)


def kernel(
    tok, gate_in, gate_slots, up_in, up_slots, down_in, down_slots, counts, out,
    gate_w, up_w, down_w, first, xs, acc, esend, erecv, hid, r0, r1, s2, r2, s3, r3, tab_v, tab_o, tab,
    w_sem, w_send, w_recv, t_send, t_recv, t_sem, a1s, a1r, a2s, a2r, a3s, a3r, a4s, a4r, es, er, hs, hr,
    b0s, b0r, b1s, b1r, b2s, b2r, b3s, b3r,
):
    s, t = lax.axis_index("seq"), lax.axis_index("tensor")
    yl, core = lax.div(s, 2), lax.rem(s, 2)
    z, x, yh = lax.div(t, 8), lax.rem(lax.div(t, 2), 4), lax.rem(t, 2)
    here = {"z": z, "x": x, "y": yh * 2 + yl, "core": core}

    def device(**moved):
        c = {**here, **moved}
        return (lax.rem(c["y"], 2) * 2 + c["core"], c["z"] * 8 + c["x"] * 2 + lax.div(c["y"], 2))

    def at(axis, off):
        return lax.rem(here[axis] + off, 4)

    def along(axis, off):
        return device(**{axis: at(axis, off)})

    mate = device(core=1 - core)
    pair = device(y=yh * 2 + (1 - yl))
    started = {}

    def remote(src, dst, send, recv, dev):
        return pltpu.make_async_remote_copy(
            src_ref=src, dst_ref=dst, send_sem=send, recv_sem=recv, device_id=dev, device_id_type=MESH
        )

    def start(*args):
        c = remote(*args)
        c.start()
        started[id(c)] = c
        return c

    barrier = pltpu.get_barrier_semaphore()
    for dev in [mate] + [along(a, o) for a in "xyz" for o in (1, 2, 3)]:
        pl.semaphore_signal(barrier, inc=1, device_id=dev, device_id_type=MESH)
    pl.semaphore_wait(barrier, 10)

    gather1, gather2, gather3, gather4 = {}, {}, {}, {}
    for p in PARTS:
        d1 = AXES[p][0]
        cols = pl.ds(FIRST[p] * TILE, TILES[p] * TILE)
        for o in (1, 2, 3):
            gather1[p, o] = start(
                tok.at[:, cols], first[p].at[here[d1]], a1s.at[p, o - 1], a1r.at[p, o - 1], along(d1, o)
            )
    weights = ((gate_in, gate_w), (up_in, up_w), (down_in, down_w))
    local, swap = [], []
    for m, (src, dst) in enumerate(weights):
        local.append(pltpu.make_async_copy(src.at[0], dst.at[pl.ds(0, OWN)], w_sem.at[m]))
        swap.append(remote(src.at[0], dst.at[pl.ds(OWN, OWN)], w_send.at[m], w_recv.at[m], mate))
        local[m].start()
        swap[m].start()
        dst[NONE] = jnp.zeros((BLK, BLK), BF16)

    places = lax.broadcasted_iota(jnp.int32, (8, 128), 0) * 128 + lax.broadcasted_iota(jnp.int32, (8, 128), 1)

    def tables():
        for m, slots in enumerate((gate_slots, up_slots, down_slots)):
            live = counts[0, m] - s * OWN

            def enter(j, table, m=m, slots=slots, live=live):
                i = slots[0, j]
                if m < 2:
                    place = lax.rem(i, COLS) * 128 + lax.div(i, COLS)
                else:
                    place = lax.div(i, 64) * 128 + lax.rem(i, 64)
                return jnp.where((places == place) & (j < live), j, table)

            tab_v[m] = lax.fori_loop(0, OWN, enter, jnp.full((8, 128), NONE, jnp.int32))

    for p in PARTS:
        first[p][here[AXES[p][0]]] = tok[:, FIRST[p] * TILE : (FIRST[p] + TILES[p]) * TILE]

    def start_gather2(h, p):
        d1, d2, d3 = AXES[p]
        part = xs[p].at[h, :, here[d3], here[d2]]
        for o in (1, 2, 3):
            gather2[h, p, o] = start(part, part, a2s.at[h, p, o - 1], a2r.at[h, p, o - 1], along(d2, o))

    for p in PARTS:
        d1, d2, d3 = AXES[p]
        for o in (1, 2, 3):
            gather1[p, o].wait_recv()

        def regroup(n, _, p=p, d2=d2, d3=d3):
            cols = pl.ds(pl.multiple_of(n * TILE, TILE), TILE)
            rows = [first[p][q, :, cols].astype(F32) for q in range(4)]
            top, end = swap4(rows[0], rows[1]), swap4(rows[2], rows[3])
            for h in range(HALVES):
                xs[p][h, n, here[d3], here[d2]] = jnp.concatenate([top[h], end[h]], 0).astype(BF16)
            return 0

        lax.fori_loop(0, TILES[p], regroup, 0)
        start_gather2(0, p)
    for p in PARTS:
        start_gather2(1, p)
    tables()
    swap_tab = remote(tab_v, tab_o, t_send.at[0], t_recv.at[0], mate)
    swap_tab.start()

    def start_gather3(h, p):
        d3 = AXES[p][2]
        for o in (1, 2, 3):
            gather2[h, p, o].wait_recv()
        part = xs[p].at[h, :, here[d3]]
        for i, o in enumerate((1, 3)):
            gather3[h, p, i] = start(part, part, a3s.at[h, p, i], a3r.at[h, p, i], along(d3, o))

    def start_gather4(h, p):
        d3 = AXES[p][2]
        for i, o in enumerate((1, 3)):
            gather3[h, p, i].wait_recv()
            part = xs[p].at[h, :, at(d3, 4 - o), pl.ds(2 * i, 2)]
            gather4[h, p, i] = start(part, part, a4s.at[h, p, i], a4r.at[h, p, i], along(d3, o))

    for p in PARTS:
        start_gather3(0, p)
    for p in PARTS:
        start_gather4(0, p)
    for p in PARTS:
        start_gather3(1, p)

    swap_tab.wait()
    tab_v[...] = jnp.minimum(tab_v[...], tab_o[...] + OWN)
    to_scalar = pltpu.make_async_copy(tab_v, tab, t_sem.at[0])
    to_scalar.start()
    to_scalar.wait()
    for m in range(3):
        local[m].wait()
        swap[m].wait()

    def project(p, h, j):
        left = jnp.concatenate([xs[p][h, n].reshape(256, TILE) for n in range(TILES[p])], 1)
        rows = []
        for r in range(2 * FIRST[p], 2 * (FIRST[p] + TILES[p])):
            rows.append(jnp.concatenate([gate_w[tab[0, j, r]], up_w[tab[1, j, r]]], 1))
        acc[j, p] = jnp.dot(left, jnp.concatenate(rows, 0), preferred_element_type=F32).reshape(32, 8, TILE)

    def sums(j, kz, kx):
        tiles = {}
        for ky in range(2):
            v = {}
            for i in range(2):
                zz, xx = 2 * kz + i, 2 * kx + i
                y0, y1 = (acc[j, 1, ((2 * ky + k) * 4 + zz) * 2 + kx] for k in range(2))
                v[1, i, 0], v[1, i, 1] = swap4(y0, y1)
                y0, y1 = (acc[j, 2, (xx * 4 + 2 * ky + k) * 2 + kz] for k in range(2))
                v[2, 0, i], v[2, 1, i] = swap4(y0, y1)
            for i in range(2):
                for k in range(2):
                    own = acc[j, 0, ((2 * kz + i) * 4 + 2 * kx + k) * 2 + ky]
                    tiles[i, k, ky] = own + v[1, i, k] + v[2, i, k]
        return {(i, k): jnp.concatenate([tiles[i, k, 0], tiles[i, k, 1]], 0) for i in range(2) for k in range(2)}

    def exchange(h, j):
        return remote(esend.at[h, j], erecv.at[h, j], es.at[h, j], er.at[h, j], pair)

    def give(h, j):
        mine = hid.at[h, 0, j, pl.ds(yl * 8, 8)]
        return remote(mine, mine, hs.at[h, j], hr.at[h, j], pair)

    def project_all(h, lo, hi):
        def body(j, _):
            for p in PARTS:
                project(p, h, j)
            for kx in range(2):
                for (i, k), v in sums(j, 1 - yl, kx).items():
                    esend[h, j, i * 4 + 2 * kx + k] = v.astype(BF16)
            exchange(h, j).start()
            return 0

        lax.fori_loop(lo, hi, body, 0)

    def finish(h):
        def body(j, _):
            exchange(h, j).wait_recv()
            for kx in range(2):
                for (i, k), v in sums(j, yl, kx).items():
                    row = i * 4 + 2 * kx + k
                    v = v + erecv[h, j, row].astype(F32)
                    g, u = v[:, :BLK], v[:, BLK:]
                    hid[h, 0, j, yl * 8 + row] = (g / (1.0 + jnp.exp(-g)) * u).astype(BF16)
            give(h, j).start()
            return 0

        lax.fori_loop(0, COLS, body, 0)

    def reorder(h):
        def body(j, _):
            give(h, j).wait_recv()
            v = hid[h, 0, j].astype(F32)

            def group(zz, xx, ky):
                return v[zz * 4 + xx, 8 * ky : 8 * ky + 8]

            for ky in range(2):
                for i in range(4):
                    a = [swap4(group(i, 2 * k, ky), group(i, 2 * k + 1, ky)) for k in range(2)]
                    b = [swap4(group(2 * k, i, ky), group(2 * k + 1, i, ky)) for k in range(2)]
                    for k in range(2):
                        yy = 2 * ky + k
                        hid[h, 1, j, yy * 4 + i] = jnp.concatenate([a[0][k], a[1][k]], 0).astype(BF16)
                        hid[h, 2, j, i * 4 + yy] = jnp.concatenate([b[0][k], b[1][k]], 0).astype(BF16)
            return 0

        lax.fori_loop(0, COLS, body, 0)

    scatter0, scatter1, scatter2, scatter3 = {}, {}, {}, {}

    def span(p, c):
        a, b = CUTS[p][c : c + 2]
        return a, b, pl.ds(a, b - a)

    def down(h, p, c):
        d3 = AXES[p][2]
        a, b, tiles = span(p, c)
        left = jnp.concatenate([hid[h, p, j].reshape(256, BLK) for j in range(COLS)], 1)
        for n in range(a, b):
            col = 2 * (FIRST[p] + n)
            rows = []
            for j in range(COLS):
                rows.append(jnp.concatenate([down_w[tab[2, j, col]], down_w[tab[2, j, col + 1]]], 1))
            v = jnp.dot(left, jnp.concatenate(rows, 0), preferred_element_type=F32)
            xs[p][h, n] = v.astype(BF16).reshape(4, 4, 16, TILE)
        for i, o in enumerate((1, 3)):
            src = xs[p].at[h, tiles, at(d3, 2), pl.ds(2 * i, 2)]
            scatter0[h, p, c, i] = start(
                src, r0[p].at[h, i, tiles], b0s.at[h, c, p, i], b0r.at[h, c, p, i], along(d3, o)
            )

    def pass_on(h, p, c):
        d3 = AXES[p][2]
        a, b, tiles = span(p, c)
        for i, o in enumerate((1, 3)):
            scatter0[h, p, c, i].wait_recv()

            def body(n, _, i=i, o=o):
                dst = xs[p].at[h, n, at(d3, o), pl.ds(2 * i, 2)]
                dst[...] = (dst[...].astype(F32) + r0[p][h, i, n].astype(F32)).astype(BF16)
                return 0

            lax.fori_loop(a, b, body, 0)
            src = xs[p].at[h, tiles, at(d3, o)]
            scatter1[h, p, c, i] = start(
                src, r1[p].at[h, i, tiles], b1s.at[h, c, p, i], b1r.at[h, c, p, i], along(d3, o)
            )

    def add1(h, p, c):
        d2, d3 = AXES[p][1:]
        a, b, tiles = span(p, c)
        for i in range(2):
            scatter1[h, p, c, i].wait_recv()

        def body(n, _):
            v = xs[p][h, n, here[d3]].astype(F32) + r1[p][h, 0, n].astype(F32) + r1[p][h, 1, n].astype(F32)
            s2[p][h, n] = v.astype(BF16)
            return 0

        lax.fori_loop(a, b, body, 0)
        for o in (1, 2, 3):
            src = s2[p].at[h, tiles, at(d2, o)]
            scatter2[h, p, c, o] = start(
                src, r2[p].at[h, o - 1, tiles], b2s.at[h, c, p, o - 1], b2r.at[h, c, p, o - 1], along(d2, o)
            )

    def sum2(h, p, n):
        v = s2[p][h, n, here[AXES[p][1]]].astype(F32)
        for o in range(3):
            v = v + r2[p][h, o, n].astype(F32)
        return v

    def add2(p, c):
        d1 = AXES[p][0]
        a, b, tiles = span(p, c)
        for h in range(HALVES):
            for o in (1, 2, 3):
                scatter2[h, p, c, o].wait_recv()

        def body(n, _):
            a, b = sum2(0, p, n), sum2(1, p, n)
            for k in range(2):
                u, v = swap4(a[8 * k : 8 * k + 8], b[8 * k : 8 * k + 8])
                s3[p][n, 2 * k] = u
                s3[p][n, 2 * k + 1] = v
            return 0

        lax.fori_loop(a, b, body, 0)
        for o in (1, 2, 3):
            src = s3[p].at[tiles, at(d1, o)]
            scatter3[p, c, o] = start(
                src, r3[p].at[o - 1, tiles], b3s.at[c, p, o - 1], b3r.at[c, p, o - 1], along(d1, o)
            )

    def add3(p, c):
        d1 = AXES[p][0]
        a, b, tiles = span(p, c)
        for o in (1, 2, 3):
            scatter3[p, c, o].wait_recv()

        def body(n, _):
            v = s3[p][n, here[d1]] + r3[p][0, n] + r3[p][1, n] + r3[p][2, n]
            out[:, pl.ds(pl.multiple_of((FIRST[p] + n) * TILE, TILE), TILE)] = v.astype(BF16)
            return 0

        lax.fori_loop(a, b, body, 0)

    def end_gather4(h):
        for p in PARTS:
            for i in range(2):
                gather4[h, p, i].wait_recv()

    def end_sends(h):
        for p in PARTS:
            for o in (1, 2, 3):
                done(gather2[h, p, o])
            for i in range(2):
                done(gather3[h, p, i])
                done(gather4[h, p, i])

    def done(c):
        c.wait_send()
        del started[id(c)]

    def each(step, *args):
        for c in range(CHUNKS):
            for p in PARTS:
                step(*args, p, c)

    end_gather4(0)
    project_all(0, 0, 4)
    for p in PARTS:
        start_gather4(1, p)
    project_all(0, 4, COLS)
    finish(0)
    end_gather4(1)
    project_all(1, 0, COLS)
    reorder(0)
    end_sends(0)
    each(down, 0)
    finish(1)
    each(pass_on, 0)
    reorder(1)
    end_sends(1)
    each(down, 1)
    each(add1, 0)
    each(pass_on, 1)
    each(add1, 1)
    each(add2)
    each(add3)

    def sent(j, _):
        for h in range(HALVES):
            exchange(h, j).wait_send()
            give(h, j).wait_send()
        return 0

    lax.fori_loop(0, COLS, sent, 0)
    for c in started.values():
        c.wait_send()


def on_device(tokens, gate_blocks, gate_slots, up_blocks, up_slots, down_blocks, down_slots, block_counts):
    vmem = pl.BlockSpec(memory_space=pltpu.VMEM)
    smem = pl.BlockSpec(memory_space=pltpu.SMEM)
    hbm = pl.BlockSpec(memory_space=pl.ANY)
    dma = pltpu.SemaphoreType.DMA

    def parts(shape, dtype):
        return [pltpu.VMEM(shape(n), dtype) for n in TILES]

    weights = pltpu.VMEM((NONE + 1, BLK, BLK), BF16)
    small, three, two, cols = dma((3,)), dma((HALVES, 3, 3)), dma((HALVES, 3, 2)), dma((HALVES, COLS))
    return pl.pallas_call(
        kernel,
        name="layer",
        out_shape=jax.ShapeDtypeStruct(tokens.shape, BF16),
        in_specs=[vmem, hbm, smem, hbm, smem, hbm, smem, smem],
        out_specs=vmem,
        scratch_shapes=[
            weights,
            weights,
            weights,
            parts(lambda n: (4, 8, n * TILE), BF16),
            parts(lambda n: (HALVES, n, 4, 4, 16, TILE), BF16),
            pltpu.VMEM((COLS, 3, 32, 8, TILE), F32),
            pltpu.VMEM((HALVES, COLS, 8, 16, TILE), BF16),
            pltpu.VMEM((HALVES, COLS, 8, 16, TILE), BF16),
            pltpu.VMEM((HALVES, 3, COLS, 16, 16, BLK), BF16),
            parts(lambda n: (HALVES, 2, n, 2, 16, TILE), BF16),
            parts(lambda n: (HALVES, 2, n, 4, 16, TILE), BF16),
            parts(lambda n: (HALVES, n, 4, 16, TILE), BF16),
            parts(lambda n: (HALVES, 3, n, 16, TILE), BF16),
            parts(lambda n: (n, 4, 8, TILE), F32),
            parts(lambda n: (3, n, 8, TILE), F32),
            pltpu.VMEM((3, 8, 128), jnp.int32),
            pltpu.VMEM((3, 8, 128), jnp.int32),
            pltpu.SMEM((3, 8, 128), jnp.int32),
            small, small, small, dma((1,)), dma((1,)), dma((1,)),
            dma((3, 3)), dma((3, 3)), three, three, two, two, two, two, cols, cols, cols, cols,
            dma((HALVES, CHUNKS, 3, 2)), dma((HALVES, CHUNKS, 3, 2)), dma((HALVES, CHUNKS, 3, 2)),
            dma((HALVES, CHUNKS, 3, 2)), dma((HALVES, CHUNKS, 3, 3)), dma((HALVES, CHUNKS, 3, 3)),
            dma((CHUNKS, 3, 3)), dma((CHUNKS, 3, 3)),
        ],
        compiler_params=pltpu.CompilerParams(
            collective_id=0, has_side_effects=True, vmem_limit_bytes=60 * 2**20
        ),
    )(tokens, gate_blocks, gate_slots, up_blocks, up_slots, down_blocks, down_slots, block_counts)


def solution(mesh):
    return jax.shard_map(
        on_device,
        mesh=mesh,
        in_specs=(
            P(("seq", "tensor"), None),
            P("tensor", "seq", None, None),
            P("tensor", "seq"),
            P("tensor", "seq", None, None),
            P("tensor", "seq"),
            P("tensor", "seq", None, None),
            P("tensor", "seq"),
            P("tensor", None),
        ),
        out_specs=P(("seq", "tensor"), None),
        check_vma=False,
    )
```

```python
import jax
import jax.numpy as jnp
from jax import lax
from jax.experimental import pallas as pl
from jax.experimental.pallas import tpu as pltpu
from jax.sharding import PartitionSpec as P

MESH = pl.DeviceIdType.MESH
BF16, F32 = jnp.bfloat16, jnp.float32
BLK = 128
TILE = 256
COLS = 7
OWN = 84
NONE = 2 * OWN
TILES = (12, 8, 12)
FIRST = (0, TILES[0], TILES[0] + TILES[1])
AXES = (("y", "x", "z"), ("x", "z", "y"), ("z", "y", "x"))
PARTS = range(3)
HALVES = 2
PIECES = ((0, 0, 6), (1, 12, 4), (2, 20, 6), (0, 6, 6), (1, 16, 4), (2, 26, 6))
ALL = range(len(PIECES))


def swap4(a, b):
    low = lax.broadcasted_iota(jnp.int32, a.shape, 0) < 4
    return jnp.where(low, a, pltpu.roll(b, 4, 0)), jnp.where(low, pltpu.roll(a, 4, 0), b)


def kernel(
    tok, gate_in, gate_slots, up_in, up_slots, down_in, down_slots, counts, out,
    gate_w, up_w, down_w, first, xs, ys, acc, esend, erecv, hid, r0, r1, s2, r2, s3, r3, tab_v, tab_o, tab,
    w_sem, w_send, w_recv, t_send, t_recv, t_sem, a1s, a1r, a2s, a2r, a3s, a3r, a4s, a4r, es, er, hs, hr,
    b0s, b0r, b1s, b1r, b2s, b2r, b3s, b3r, b4s, b4r,
):
    s, t = lax.axis_index("seq"), lax.axis_index("tensor")
    yl, core = lax.div(s, 2), lax.rem(s, 2)
    z, x, yh = lax.div(t, 8), lax.rem(lax.div(t, 2), 4), lax.rem(t, 2)
    here = {"z": z, "x": x, "y": yh * 2 + yl, "core": core}

    def device(**moved):
        c = {**here, **moved}
        return (lax.rem(c["y"], 2) * 2 + c["core"], c["z"] * 8 + c["x"] * 2 + lax.div(c["y"], 2))

    def at(axis, off):
        return lax.rem(here[axis] + off, 4)

    def along(axis, off):
        return device(**{axis: at(axis, off)})

    mate = device(core=1 - core)
    pair = device(y=yh * 2 + (1 - yl))
    started = {}

    def remote(src, dst, send, recv, dev):
        return pltpu.make_async_remote_copy(
            src_ref=src, dst_ref=dst, send_sem=send, recv_sem=recv, device_id=dev, device_id_type=MESH
        )

    def start(*args):
        c = remote(*args)
        c.start()
        started[id(c)] = c
        return c

    barrier = pltpu.get_barrier_semaphore()
    for dev in [mate] + [along(a, o) for a in "xyz" for o in (1, 2, 3)]:
        pl.semaphore_signal(barrier, inc=1, device_id=dev, device_id_type=MESH)
    pl.semaphore_wait(barrier, 10)

    gather1, gather2, gather3, gather4 = {}, {}, {}, {}
    for p in PARTS:
        d1 = AXES[p][0]
        cols = pl.ds(FIRST[p] * TILE, TILES[p] * TILE)
        for o in (1, 2, 3):
            gather1[p, o] = start(
                tok.at[:, cols], first[p].at[here[d1]], a1s.at[p, o - 1], a1r.at[p, o - 1], along(d1, o)
            )
    weights = ((gate_in, gate_w), (up_in, up_w), (down_in, down_w))
    local, swap = [], []
    for m, (src, dst) in enumerate(weights):
        local.append(pltpu.make_async_copy(src.at[0], dst.at[pl.ds(0, OWN)], w_sem.at[m]))
        swap.append(remote(src.at[0], dst.at[pl.ds(OWN, OWN)], w_send.at[m], w_recv.at[m], mate))
        local[m].start()
        if m < 2:
            swap[m].start()
        dst[NONE] = jnp.zeros((BLK, BLK), BF16)

    places = lax.broadcasted_iota(jnp.int32, (8, 128), 0) * 128 + lax.broadcasted_iota(jnp.int32, (8, 128), 1)

    def tables():
        for m, slots in enumerate((gate_slots, up_slots, down_slots)):
            live = counts[0, m] - s * OWN

            def enter(j, table, m=m, slots=slots, live=live):
                i = slots[0, j]
                if m < 2:
                    place = lax.rem(i, COLS) * 128 + lax.div(i, COLS)
                else:
                    place = lax.div(i, 64) * 128 + lax.rem(i, 64)
                return jnp.where((places == place) & (j < live), j, table)

            tab_v[m] = lax.fori_loop(0, OWN, enter, jnp.full((8, 128), NONE, jnp.int32))

    for p in PARTS:
        first[p][here[AXES[p][0]]] = tok[:, FIRST[p] * TILE : (FIRST[p] + TILES[p]) * TILE]

    def start_gather2(h, p):
        d1, d2, d3 = AXES[p]
        part = xs[p].at[h, here[d3], here[d2]]
        for o in (1, 2, 3):
            gather2[h, p, o] = start(part, part, a2s.at[h, p, o - 1], a2r.at[h, p, o - 1], along(d2, o))

    for p in PARTS:
        d1, d2, d3 = AXES[p]
        for o in (1, 2, 3):
            gather1[p, o].wait_recv()

        def regroup(n, _, p=p, d2=d2, d3=d3):
            cols = pl.ds(pl.multiple_of(n * TILE, TILE), TILE)
            rows = [first[p][q, :, cols].astype(F32) for q in range(4)]
            top, end = swap4(rows[0], rows[1]), swap4(rows[2], rows[3])
            for h in range(HALVES):
                xs[p][h, here[d3], here[d2], n] = jnp.concatenate([top[h], end[h]], 0).astype(BF16)
            return 0

        lax.fori_loop(0, TILES[p], regroup, 0)
        start_gather2(0, p)
    for p in PARTS:
        start_gather2(1, p)
    tables()
    swap_tab = remote(tab_v, tab_o, t_send.at[0], t_recv.at[0], mate)
    swap_tab.start()

    def start_gather3(h, p):
        d3 = AXES[p][2]
        for o in (1, 2, 3):
            gather2[h, p, o].wait_recv()
        for k in range(2):
            for i, o in enumerate((1, 3)):
                part = xs[p].at[h, here[d3], pl.ds(2 * (k if i == 0 else 1 - k), 2)]
                gather3[h, p, i, k] = start(part, part, a3s.at[h, p, i, k], a3r.at[h, p, i, k], along(d3, o))

    def start_gather4(h, p):
        d3 = AXES[p][2]
        for i, o in enumerate((1, 3)):
            gather3[h, p, i, 0].wait_recv()
            part = xs[p].at[h, at(d3, 4 - o), pl.ds(2 * i, 2)]
            gather4[h, p, i] = start(part, part, a4s.at[h, p, i], a4r.at[h, p, i], along(d3, o))

    for p in PARTS:
        start_gather3(0, p)
    for p in PARTS:
        start_gather4(0, p)
    for p in PARTS:
        start_gather3(1, p)

    swap_tab.wait()
    tab_v[...] = jnp.minimum(tab_v[...], tab_o[...] + OWN)
    to_scalar = pltpu.make_async_copy(tab_v, tab, t_sem.at[0])
    to_scalar.start()
    to_scalar.wait()
    for m in range(2):
        local[m].wait()
        swap[m].wait()

    def project(p, h, j):
        left = jnp.concatenate([xs[p][h, :, :, n].reshape(256, TILE) for n in range(TILES[p])], 1)
        rows = []
        for r in range(2 * FIRST[p], 2 * (FIRST[p] + TILES[p])):
            rows.append(jnp.concatenate([gate_w[tab[0, j, r]], up_w[tab[1, j, r]]], 1))
        acc[j, p] = jnp.dot(left, jnp.concatenate(rows, 0), preferred_element_type=F32).reshape(32, 8, TILE)

    def sums(j, kz, kx):
        tiles = {}
        for ky in range(2):
            v = {}
            for i in range(2):
                zz, xx = 2 * kz + i, 2 * kx + i
                y0, y1 = (acc[j, 1, ((2 * ky + k) * 4 + zz) * 2 + kx] for k in range(2))
                v[1, i, 0], v[1, i, 1] = swap4(y0, y1)
                y0, y1 = (acc[j, 2, (xx * 4 + 2 * ky + k) * 2 + kz] for k in range(2))
                v[2, 0, i], v[2, 1, i] = swap4(y0, y1)
            for i in range(2):
                for k in range(2):
                    own = acc[j, 0, ((2 * kz + i) * 4 + 2 * kx + k) * 2 + ky]
                    tiles[i, k, ky] = own + v[1, i, k] + v[2, i, k]
        return {(i, k): jnp.concatenate([tiles[i, k, 0], tiles[i, k, 1]], 0) for i in range(2) for k in range(2)}

    def exchange(h, j):
        return remote(esend.at[h, j], erecv.at[h, j], es.at[h, j], er.at[h, j], pair)

    def give(h, j):
        mine = hid.at[h, 0, j, pl.ds(yl * 8, 8)]
        return remote(mine, mine, hs.at[h, j], hr.at[h, j], pair)

    def project_all(h, lo, hi):
        def body(j, _):
            for p in PARTS:
                project(p, h, j)
            for kx in range(2):
                for (i, k), v in sums(j, 1 - yl, kx).items():
                    esend[h, j, i * 4 + 2 * kx + k] = v.astype(BF16)
            exchange(h, j).start()
            return 0

        lax.fori_loop(lo, hi, body, 0)

    def finish(h):
        def body(j, _):
            exchange(h, j).wait_recv()
            for kx in range(2):
                for (i, k), v in sums(j, yl, kx).items():
                    row = i * 4 + 2 * kx + k
                    v = v + erecv[h, j, row].astype(F32)
                    g, u = v[:, :BLK], v[:, BLK:]
                    hid[h, 0, j, yl * 8 + row] = (g / (1.0 + jnp.exp(-g)) * u).astype(BF16)
            give(h, j).start()
            return 0

        lax.fori_loop(0, COLS, body, 0)

    def reorder(h):
        def body(j, _):
            give(h, j).wait_recv()
            v = hid[h, 0, j].astype(F32)

            def group(zz, xx, ky):
                return v[zz * 4 + xx, 8 * ky : 8 * ky + 8]

            for ky in range(2):
                for i in range(4):
                    a = [swap4(group(i, 2 * k, ky), group(i, 2 * k + 1, ky)) for k in range(2)]
                    b = [swap4(group(2 * k, i, ky), group(2 * k + 1, i, ky)) for k in range(2)]
                    for k in range(2):
                        yy = 2 * ky + k
                        hid[h, 1, j, yy * 4 + i] = jnp.concatenate([a[0][k], a[1][k]], 0).astype(BF16)
                        hid[h, 2, j, i * 4 + yy] = jnp.concatenate([b[0][k], b[1][k]], 0).astype(BF16)
            return 0

        lax.fori_loop(0, COLS, body, 0)

    scatter0, scatter1, scatter2, scatter3, scatter4 = {}, {}, {}, {}, {}

    def down(h, q):
        p, a, tiles = PIECES[q]
        d3 = AXES[p][2]
        left = jnp.concatenate([hid[h, p, j].reshape(256, BLK) for j in range(COLS)], 1)
        for n in range(tiles):
            col = 2 * (a + n)
            rows = []
            for j in range(COLS):
                rows.append(jnp.concatenate([down_w[tab[2, j, col]], down_w[tab[2, j, col + 1]]], 1))
            v = jnp.dot(left, jnp.concatenate(rows, 0), preferred_element_type=F32)
            ys[q][h, :, :, n] = v.astype(BF16).reshape(4, 4, 16, TILE)
        for i, o in enumerate((1, 3)):
            src = ys[q].at[h, at(d3, 2), pl.ds(2 * i, 2)]
            scatter0[h, q, i] = start(src, r0[q].at[h, i], b0s.at[h, q, i], b0r.at[h, q, i], along(d3, o))
        for i, o in enumerate((1, 3)):
            ready = pl.ds(2 - 2 * i, 2)
            src = ys[q].at[h, at(d3, o), ready]
            scatter4[h, q, i] = start(src, r1[q].at[h, i, ready], b4s.at[h, q, i], b4r.at[h, q, i], along(d3, o))

    def pass_on(h, q):
        p, a, tiles = PIECES[q]
        d3 = AXES[p][2]
        for i, o in enumerate((1, 3)):
            scatter0[h, q, i].wait_recv()

            def body(n, _, i=i, o=o):
                for k in range(2):
                    v = ys[q][h, at(d3, o), 2 * i + k, n].astype(F32) + r0[q][h, i, k, n].astype(F32)
                    ys[q][h, at(d3, o), 2 * i + k, n] = v.astype(BF16)
                return 0

            lax.fori_loop(0, tiles, body, 0)
            rest = pl.ds(2 * i, 2)
            src = ys[q].at[h, at(d3, o), rest]
            scatter1[h, q, i] = start(src, r1[q].at[h, i, rest], b1s.at[h, q, i], b1r.at[h, q, i], along(d3, o))

    def sum1(h, q, k, n):
        v = ys[q][h, here[AXES[PIECES[q][0]][2]], k, n].astype(F32)
        return v + r1[q][h, 0, k, n].astype(F32) + r1[q][h, 1, k, n].astype(F32)

    def add1(h, q):
        p, a, tiles = PIECES[q]
        d2 = AXES[p][1]
        for i in range(2):
            scatter1[h, q, i].wait_recv()
            scatter4[h, q, i].wait_recv()

        def body(n, _):
            for k in range(4):
                s2[q][h, k, n] = sum1(h, q, k, n).astype(BF16)
            return 0

        lax.fori_loop(0, tiles, body, 0)
        for o in (1, 2, 3):
            src = s2[q].at[h, at(d2, o)]
            scatter2[h, q, o] = start(src, r2[q].at[h, o - 1], b2s.at[h, q, o - 1], b2r.at[h, q, o - 1], along(d2, o))

    def sum2(h, q, n):
        v = sum1(h, q, here[AXES[PIECES[q][0]][1]], n)
        for o in range(3):
            v = v + r2[q][h, o, n].astype(F32)
        return v

    def add2(h, q):
        p, a, tiles = PIECES[q]
        d1 = AXES[p][0]
        for o in (1, 2, 3):
            scatter2[h, q, o].wait_recv()

        def body(n, _):
            a, b = sum2(h, q, 2 * n), sum2(h, q, 2 * n + 1)
            for k in range(2):
                u, v = swap4(a[8 * k : 8 * k + 8], b[8 * k : 8 * k + 8])
                s3[q][h, 2 * k, n] = u
                s3[q][h, 2 * k + 1, n] = v
            return 0

        lax.fori_loop(0, tiles // 2, body, 0)
        for o in (1, 2, 3):
            src = s3[q].at[h, at(d1, o)]
            scatter3[h, q, o] = start(src, r3[q].at[h, o - 1], b3s.at[h, q, o - 1], b3r.at[h, q, o - 1], along(d1, o))

    def add3(q):
        p, a, tiles = PIECES[q]
        d1 = AXES[p][0]
        for h in range(HALVES):
            for o in (1, 2, 3):
                scatter3[h, q, o].wait_recv()

        def body(n, _):
            v = [s3[q][h, here[d1], n] + r3[q][h, 0, n] + r3[q][h, 1, n] + r3[q][h, 2, n] for h in range(HALVES)]
            for k, rows in enumerate(swap4(*v)):
                out[:, pl.ds(pl.multiple_of((a + 2 * n + k) * TILE, TILE), TILE)] = rows.astype(BF16)
            return 0

        lax.fori_loop(0, tiles // 2, body, 0)

    def end_gather4(h):
        for p in PARTS:
            for i in range(2):
                gather3[h, p, i, 1].wait_recv()
                gather4[h, p, i].wait_recv()

    def each(step, *args):
        for q in ALL:
            step(*args, q)

    end_gather4(0)
    project_all(0, 0, 4)
    for p in PARTS:
        start_gather4(1, p)
    project_all(0, 4, COLS)
    finish(0)
    end_gather4(1)
    swap[2].start()
    project_all(1, 0, COLS)
    reorder(0)
    local[2].wait()
    swap[2].wait()
    each(down, 0)
    finish(1)
    each(pass_on, 0)
    reorder(1)
    each(down, 1)
    each(pass_on, 1)
    each(add1, 0)
    each(add1, 1)
    each(add2, 0)
    each(add2, 1)
    each(add3)

    def sent(j, _):
        for h in range(HALVES):
            exchange(h, j).wait_send()
            give(h, j).wait_send()
        return 0

    lax.fori_loop(0, COLS, sent, 0)
    for c in started.values():
        c.wait_send()


def on_device(tokens, gate_blocks, gate_slots, up_blocks, up_slots, down_blocks, down_slots, block_counts):
    vmem = pl.BlockSpec(memory_space=pltpu.VMEM)
    smem = pl.BlockSpec(memory_space=pltpu.SMEM)
    hbm = pl.BlockSpec(memory_space=pl.ANY)
    dma = pltpu.SemaphoreType.DMA

    def parts(shape, dtype):
        return [pltpu.VMEM(shape(n), dtype) for n in TILES]

    def pieces(shape, dtype):
        return [pltpu.VMEM(shape(n), dtype) for _, _, n in PIECES]

    weights = pltpu.VMEM((NONE + 1, BLK, BLK), BF16)
    small, three, two, cols = dma((3,)), dma((HALVES, 3, 3)), dma((HALVES, 3, 2)), dma((HALVES, COLS))
    many = len(PIECES)
    out_two, out_three = dma((HALVES, many, 2)), dma((HALVES, many, 3))
    return pl.pallas_call(
        kernel,
        name="layer",
        out_shape=jax.ShapeDtypeStruct(tokens.shape, BF16),
        in_specs=[vmem, hbm, smem, hbm, smem, hbm, smem, smem],
        out_specs=vmem,
        scratch_shapes=[
            weights,
            weights,
            weights,
            parts(lambda n: (4, 8, n * TILE), BF16),
            parts(lambda n: (HALVES, 4, 4, n, 16, TILE), BF16),
            pieces(lambda n: (HALVES, 4, 4, n, 16, TILE), BF16),
            pltpu.VMEM((COLS, 3, 32, 8, TILE), F32),
            pltpu.VMEM((HALVES, COLS, 8, 16, TILE), BF16),
            pltpu.VMEM((HALVES, COLS, 8, 16, TILE), BF16),
            pltpu.VMEM((HALVES, 3, COLS, 16, 16, BLK), BF16),
            pieces(lambda n: (HALVES, 2, 2, n, 16, TILE), BF16),
            pieces(lambda n: (HALVES, 2, 4, n, 16, TILE), BF16),
            pieces(lambda n: (HALVES, 4, n, 16, TILE), BF16),
            pieces(lambda n: (HALVES, 3, n, 16, TILE), BF16),
            pieces(lambda n: (HALVES, 4, n // 2, 8, TILE), F32),
            pieces(lambda n: (HALVES, 3, n // 2, 8, TILE), F32),
            pltpu.VMEM((3, 8, 128), jnp.int32),
            pltpu.VMEM((3, 8, 128), jnp.int32),
            pltpu.SMEM((3, 8, 128), jnp.int32),
            small, small, small, dma((1,)), dma((1,)), dma((1,)),
            dma((3, 3)), dma((3, 3)), three, three, dma((HALVES, 3, 2, 2)), dma((HALVES, 3, 2, 2)), two, two, cols, cols, cols, cols,
            out_two, out_two, out_two, out_two, out_three, out_three, out_three, out_three, out_two, out_two,
        ],
        compiler_params=pltpu.CompilerParams(
            collective_id=0, has_side_effects=True, vmem_limit_bytes=60 * 2**20
        ),
    )(tokens, gate_blocks, gate_slots, up_blocks, up_slots, down_blocks, down_slots, block_counts)


def solution(mesh):
    return jax.shard_map(
        on_device,
        mesh=mesh,
        in_specs=(
            P(("seq", "tensor"), None),
            P("tensor", "seq", None, None),
            P("tensor", "seq"),
            P("tensor", "seq", None, None),
            P("tensor", "seq"),
            P("tensor", "seq", None, None),
            P("tensor", "seq"),
            P("tensor", None),
        ),
        out_specs=P(("seq", "tensor"), None),
        check_vma=False,
    )
```

```python
import jax
import jax.numpy as jnp
from jax import lax
from jax.experimental import pallas as pl
from jax.experimental.pallas import tpu as pltpu
from jax.sharding import PartitionSpec as P

MESH = pl.DeviceIdType.MESH
BF16, F32 = jnp.bfloat16, jnp.float32
BLK = 128
TILE = 256
COLS = 7
OWN = 84
NONE = 2 * OWN
TILES = (12, 8, 12)
FIRST = (0, TILES[0], TILES[0] + TILES[1])
AXES = (("y", "x", "z"), ("x", "z", "y"), ("z", "y", "x"))
PARTS = range(3)
HALVES = 2
PIECES = ((0, 0, 6), (1, 12, 4), (2, 20, 6), (0, 6, 6), (1, 16, 4), (2, 26, 6))
ALL = range(len(PIECES))


def swap4(a, b):
    low = lax.broadcasted_iota(jnp.int32, a.shape, 0) < 4
    return jnp.where(low, a, pltpu.roll(b, 4, 0)), jnp.where(low, pltpu.roll(a, 4, 0), b)


def kernel(
    tok, gate_in, gate_slots_in, up_in, up_slots_in, down_in, down_slots_in, counts_in, out,
    gate_w, up_w, down_w, first, xs, ys, acc, esend, erecv, hid, r0, r1, s2, r2, s3, r3, tab_v, tab_o, tab,
    w_sem, w_send, w_recv, t_send, t_recv, t_sem, a1s, a1r, a2s, a2r, a3s, a3r, a4s, a4r, es, er, hs, hr,
    b0s, b0r, b1s, b1r, b2s, b2r, b3s, b3r, b4s, b4r,
    gate_slots, up_slots, down_slots, counts, slot_sem, tok_sem,
):
    s, t = lax.axis_index("seq"), lax.axis_index("tensor")
    yl, core = lax.div(s, 2), lax.rem(s, 2)
    z, x, yh = lax.div(t, 8), lax.rem(lax.div(t, 2), 4), lax.rem(t, 2)
    here = {"z": z, "x": x, "y": yh * 2 + yl, "core": core}

    def device(**moved):
        c = {**here, **moved}
        return (lax.rem(c["y"], 2) * 2 + c["core"], c["z"] * 8 + c["x"] * 2 + lax.div(c["y"], 2))

    def at(axis, off):
        return lax.rem(here[axis] + off, 4)

    def along(axis, off):
        return device(**{axis: at(axis, off)})

    mate = device(core=1 - core)
    pair = device(y=yh * 2 + (1 - yl))
    started = {}

    def remote(src, dst, send, recv, dev):
        return pltpu.make_async_remote_copy(
            src_ref=src, dst_ref=dst, send_sem=send, recv_sem=recv, device_id=dev, device_id_type=MESH
        )

    def start(*args):
        c = remote(*args)
        c.start()
        started[id(c)] = c
        return c

    barrier = pltpu.get_barrier_semaphore()
    for dev in [mate] + [along(a, o) for a in "xyz" for o in (1, 2, 3)]:
        pl.semaphore_signal(barrier, inc=1, device_id=dev, device_id_type=MESH)
    loads = []
    for p in PARTS:
        cols = pl.ds(FIRST[p] * TILE, TILES[p] * TILE)
        loads.append(pltpu.make_async_copy(tok.at[:, cols], first[p].at[here[AXES[p][0]]], tok_sem.at[p]))
    slot_loads = [
        pltpu.make_async_copy(src, dst, slot_sem.at[i])
        for i, (src, dst) in enumerate(
            ((gate_slots_in, gate_slots), (up_slots_in, up_slots), (down_slots_in, down_slots), (counts_in, counts))
        )
    ]
    for c in loads + slot_loads:
        c.start()
    pl.semaphore_wait(barrier, 10)

    gather1, gather2, gather3, gather4 = {}, {}, {}, {}
    for p in PARTS:
        d1 = AXES[p][0]
        cols = pl.ds(FIRST[p] * TILE, TILES[p] * TILE)
        for o in (1, 2, 3):
            gather1[p, o] = start(
                tok.at[:, cols], first[p].at[here[d1]], a1s.at[p, o - 1], a1r.at[p, o - 1], along(d1, o)
            )
    weights = ((gate_in, gate_w), (up_in, up_w), (down_in, down_w))
    local, swap = [], []
    for m, (src, dst) in enumerate(weights):
        local.append(pltpu.make_async_copy(src.at[0], dst.at[pl.ds(0, OWN)], w_sem.at[m]))
        swap.append(remote(src.at[0], dst.at[pl.ds(OWN, OWN)], w_send.at[m], w_recv.at[m], mate))
        local[m].start()
        if m < 2:
            swap[m].start()
        dst[NONE] = jnp.zeros((BLK, BLK), BF16)

    places = lax.broadcasted_iota(jnp.int32, (8, 128), 0) * 128 + lax.broadcasted_iota(jnp.int32, (8, 128), 1)

    def tables():
        for m, slots in enumerate((gate_slots, up_slots, down_slots)):
            live = counts[0, m] - s * OWN

            def enter(j, table, m=m, slots=slots, live=live):
                i = slots[0, j]
                if m < 2:
                    place = lax.rem(i, COLS) * 128 + lax.div(i, COLS)
                else:
                    place = lax.div(i, 64) * 128 + lax.rem(i, 64)
                return jnp.where((places == place) & (j < live), j, table)

            tab_v[m] = lax.fori_loop(0, OWN, enter, jnp.full((8, 128), NONE, jnp.int32))

    def start_gather2(h, p):
        d1, d2, d3 = AXES[p]
        part = xs[p].at[h, here[d3], here[d2]]
        for o in (1, 2, 3):
            gather2[h, p, o] = start(part, part, a2s.at[h, p, o - 1], a2r.at[h, p, o - 1], along(d2, o))

    for p in PARTS:
        d1, d2, d3 = AXES[p]
        for o in (1, 2, 3):
            gather1[p, o].wait_recv()
        loads[p].wait()

        def regroup(n, _, p=p, d2=d2, d3=d3):
            cols = pl.ds(pl.multiple_of(n * TILE, TILE), TILE)
            rows = [first[p][q, :, cols].astype(F32) for q in range(4)]
            top, end = swap4(rows[0], rows[1]), swap4(rows[2], rows[3])
            for h in range(HALVES):
                xs[p][h, here[d3], here[d2], n] = jnp.concatenate([top[h], end[h]], 0).astype(BF16)
            return 0

        lax.fori_loop(0, TILES[p], regroup, 0)
        start_gather2(0, p)
    for p in PARTS:
        start_gather2(1, p)
    for c in slot_loads:
        c.wait()
    tables()
    swap_tab = remote(tab_v, tab_o, t_send.at[0], t_recv.at[0], mate)
    swap_tab.start()

    def start_gather3(h, p):
        d3 = AXES[p][2]
        for o in (1, 2, 3):
            gather2[h, p, o].wait_recv()
        for k in range(2):
            for i, o in enumerate((1, 3)):
                part = xs[p].at[h, here[d3], pl.ds(2 * (k if i == 0 else 1 - k), 2)]
                gather3[h, p, i, k] = start(part, part, a3s.at[h, p, i, k], a3r.at[h, p, i, k], along(d3, o))

    def start_gather4(h, p):
        d3 = AXES[p][2]
        for i, o in enumerate((1, 3)):
            gather3[h, p, i, 0].wait_recv()
            part = xs[p].at[h, at(d3, 4 - o), pl.ds(2 * i, 2)]
            gather4[h, p, i] = start(part, part, a4s.at[h, p, i], a4r.at[h, p, i], along(d3, o))

    for p in PARTS:
        start_gather3(0, p)
    for p in PARTS:
        start_gather4(0, p)
    for p in PARTS:
        start_gather3(1, p)

    swap_tab.wait()
    tab_v[...] = jnp.minimum(tab_v[...], tab_o[...] + OWN)
    to_scalar = pltpu.make_async_copy(tab_v, tab, t_sem.at[0])
    to_scalar.start()
    to_scalar.wait()
    for m in range(2):
        local[m].wait()
        swap[m].wait()

    def project(p, h, j):
        left = jnp.concatenate([xs[p][h, :, :, n].reshape(256, TILE) for n in range(TILES[p])], 1)
        rows = []
        for r in range(2 * FIRST[p], 2 * (FIRST[p] + TILES[p])):
            rows.append(jnp.concatenate([gate_w[tab[0, j, r]], up_w[tab[1, j, r]]], 1))
        acc[j, p] = jnp.dot(left, jnp.concatenate(rows, 0), preferred_element_type=F32).reshape(32, 8, TILE)

    def sums(j, kz, kx):
        tiles = {}
        for ky in range(2):
            v = {}
            for i in range(2):
                zz, xx = 2 * kz + i, 2 * kx + i
                y0, y1 = (acc[j, 1, ((2 * ky + k) * 4 + zz) * 2 + kx] for k in range(2))
                v[1, i, 0], v[1, i, 1] = swap4(y0, y1)
                y0, y1 = (acc[j, 2, (xx * 4 + 2 * ky + k) * 2 + kz] for k in range(2))
                v[2, 0, i], v[2, 1, i] = swap4(y0, y1)
            for i in range(2):
                for k in range(2):
                    own = acc[j, 0, ((2 * kz + i) * 4 + 2 * kx + k) * 2 + ky]
                    tiles[i, k, ky] = own + v[1, i, k] + v[2, i, k]
        return {(i, k): jnp.concatenate([tiles[i, k, 0], tiles[i, k, 1]], 0) for i in range(2) for k in range(2)}

    def exchange(h, j):
        return remote(esend.at[h, j], erecv.at[h, j], es.at[h, j], er.at[h, j], pair)

    def give(h, j):
        mine = hid.at[h, 0, j, pl.ds(yl * 8, 8)]
        return remote(mine, mine, hs.at[h, j], hr.at[h, j], pair)

    def project_all(h, lo, hi):
        def body(j, _):
            for p in PARTS:
                project(p, h, j)
            for kx in range(2):
                for (i, k), v in sums(j, 1 - yl, kx).items():
                    esend[h, j, i * 4 + 2 * kx + k] = v.astype(BF16)
            exchange(h, j).start()
            return 0

        lax.fori_loop(lo, hi, body, 0)

    def finish(h):
        def body(j, _):
            exchange(h, j).wait_recv()
            for kx in range(2):
                for (i, k), v in sums(j, yl, kx).items():
                    row = i * 4 + 2 * kx + k
                    v = v + erecv[h, j, row].astype(F32)
                    g, u = v[:, :BLK], v[:, BLK:]
                    hid[h, 0, j, yl * 8 + row] = (g / (1.0 + jnp.exp(-g)) * u).astype(BF16)
            give(h, j).start()
            return 0

        lax.fori_loop(0, COLS, body, 0)

    def reorder(h):
        def body(j, _):
            give(h, j).wait_recv()
            v = hid[h, 0, j].astype(F32)

            def group(zz, xx, ky):
                return v[zz * 4 + xx, 8 * ky : 8 * ky + 8]

            for ky in range(2):
                for i in range(4):
                    a = [swap4(group(i, 2 * k, ky), group(i, 2 * k + 1, ky)) for k in range(2)]
                    b = [swap4(group(2 * k, i, ky), group(2 * k + 1, i, ky)) for k in range(2)]
                    for k in range(2):
                        yy = 2 * ky + k
                        hid[h, 1, j, yy * 4 + i] = jnp.concatenate([a[0][k], a[1][k]], 0).astype(BF16)
                        hid[h, 2, j, i * 4 + yy] = jnp.concatenate([b[0][k], b[1][k]], 0).astype(BF16)
            return 0

        lax.fori_loop(0, COLS, body, 0)

    scatter0, scatter1, scatter2, scatter3, scatter4 = {}, {}, {}, {}, {}

    def down(h, q):
        p, a, tiles = PIECES[q]
        d3 = AXES[p][2]
        left = jnp.concatenate([hid[h, p, j].reshape(256, BLK) for j in range(COLS)], 1)
        for n in range(tiles):
            col = 2 * (a + n)
            rows = []
            for j in range(COLS):
                rows.append(jnp.concatenate([down_w[tab[2, j, col]], down_w[tab[2, j, col + 1]]], 1))
            v = jnp.dot(left, jnp.concatenate(rows, 0), preferred_element_type=F32)
            ys[q][h, :, :, n] = v.astype(BF16).reshape(4, 4, 16, TILE)
        for i, o in enumerate((1, 3)):
            src = ys[q].at[h, at(d3, 2), pl.ds(2 * i, 2)]
            scatter0[h, q, i] = start(src, r0[q].at[h, i], b0s.at[h, q, i], b0r.at[h, q, i], along(d3, o))
        for i, o in enumerate((1, 3)):
            ready = pl.ds(2 - 2 * i, 2)
            src = ys[q].at[h, at(d3, o), ready]
            scatter4[h, q, i] = start(src, r1[q].at[h, i, ready], b4s.at[h, q, i], b4r.at[h, q, i], along(d3, o))

    def pass_on(h, q):
        p, a, tiles = PIECES[q]
        d3 = AXES[p][2]
        for i, o in enumerate((1, 3)):
            scatter0[h, q, i].wait_recv()

            def body(n, _, i=i, o=o):
                for k in range(2):
                    v = ys[q][h, at(d3, o), 2 * i + k, n].astype(F32) + r0[q][h, i, k, n].astype(F32)
                    ys[q][h, at(d3, o), 2 * i + k, n] = v.astype(BF16)
                return 0

            lax.fori_loop(0, tiles, body, 0)
            rest = pl.ds(2 * i, 2)
            src = ys[q].at[h, at(d3, o), rest]
            scatter1[h, q, i] = start(src, r1[q].at[h, i, rest], b1s.at[h, q, i], b1r.at[h, q, i], along(d3, o))

    def sum1(h, q, k, n):
        v = ys[q][h, here[AXES[PIECES[q][0]][2]], k, n].astype(F32)
        return v + r1[q][h, 0, k, n].astype(F32) + r1[q][h, 1, k, n].astype(F32)

    def add1(h, q):
        p, a, tiles = PIECES[q]
        d2 = AXES[p][1]
        for i in range(2):
            scatter1[h, q, i].wait_recv()
            scatter4[h, q, i].wait_recv()

        def body(n, _):
            for k in range(4):
                s2[q][h, k, n] = sum1(h, q, k, n).astype(BF16)
            return 0

        lax.fori_loop(0, tiles, body, 0)
        for o in (1, 2, 3):
            src = s2[q].at[h, at(d2, o)]
            scatter2[h, q, o] = start(src, r2[q].at[h, o - 1], b2s.at[h, q, o - 1], b2r.at[h, q, o - 1], along(d2, o))

    def sum2(h, q, n):
        v = sum1(h, q, here[AXES[PIECES[q][0]][1]], n)
        for o in range(3):
            v = v + r2[q][h, o, n].astype(F32)
        return v

    def add2(h, q):
        p, a, tiles = PIECES[q]
        d1 = AXES[p][0]
        for o in (1, 2, 3):
            scatter2[h, q, o].wait_recv()

        def body(n, _):
            a, b = sum2(h, q, 2 * n), sum2(h, q, 2 * n + 1)
            for k in range(2):
                u, v = swap4(a[8 * k : 8 * k + 8], b[8 * k : 8 * k + 8])
                s3[q][h, 2 * k, n] = u
                s3[q][h, 2 * k + 1, n] = v
            return 0

        lax.fori_loop(0, tiles // 2, body, 0)
        for o in (1, 2, 3):
            src = s3[q].at[h, at(d1, o)]
            scatter3[h, q, o] = start(src, r3[q].at[h, o - 1], b3s.at[h, q, o - 1], b3r.at[h, q, o - 1], along(d1, o))

    def add3(q):
        p, a, tiles = PIECES[q]
        d1 = AXES[p][0]
        for h in range(HALVES):
            for o in (1, 2, 3):
                scatter3[h, q, o].wait_recv()

        def body(n, _):
            v = [s3[q][h, here[d1], n] + r3[q][h, 0, n] + r3[q][h, 1, n] + r3[q][h, 2, n] for h in range(HALVES)]
            for k, rows in enumerate(swap4(*v)):
                out[:, pl.ds(pl.multiple_of((a + 2 * n + k) * TILE, TILE), TILE)] = rows.astype(BF16)
            return 0

        lax.fori_loop(0, tiles // 2, body, 0)

    def end_gather4(h):
        for p in PARTS:
            for i in range(2):
                gather3[h, p, i, 1].wait_recv()
                gather4[h, p, i].wait_recv()

    def each(step, *args):
        for q in ALL:
            step(*args, q)

    end_gather4(0)
    project_all(0, 0, 2)
    for p in PARTS:
        start_gather4(1, p)
    project_all(0, 2, COLS)
    finish(0)
    end_gather4(1)
    swap[2].start()
    project_all(1, 0, COLS)
    reorder(0)
    local[2].wait()
    swap[2].wait()
    each(down, 0)
    finish(1)
    each(pass_on, 0)
    reorder(1)
    each(down, 1)
    each(pass_on, 1)
    each(add1, 0)
    each(add1, 1)
    each(add2, 0)
    each(add2, 1)
    each(add3)

    def sent(j, _):
        for h in range(HALVES):
            exchange(h, j).wait_send()
            give(h, j).wait_send()
        return 0

    lax.fori_loop(0, COLS, sent, 0)
    for c in started.values():
        c.wait_send()


def on_device(tokens, gate_blocks, gate_slots, up_blocks, up_slots, down_blocks, down_slots, block_counts):
    vmem = pl.BlockSpec(memory_space=pltpu.VMEM)
    hbm = pl.BlockSpec(memory_space=pl.ANY)
    dma = pltpu.SemaphoreType.DMA

    def parts(shape, dtype):
        return [pltpu.VMEM(shape(n), dtype) for n in TILES]

    def pieces(shape, dtype):
        return [pltpu.VMEM(shape(n), dtype) for _, _, n in PIECES]

    weights = pltpu.VMEM((NONE + 1, BLK, BLK), BF16)
    small, three, two, cols = dma((3,)), dma((HALVES, 3, 3)), dma((HALVES, 3, 2)), dma((HALVES, COLS))
    many = len(PIECES)
    out_two, out_three = dma((HALVES, many, 2)), dma((HALVES, many, 3))
    return pl.pallas_call(
        kernel,
        name="layer",
        out_shape=jax.ShapeDtypeStruct(tokens.shape, BF16),
        in_specs=[hbm] * 8,
        out_specs=vmem,
        scratch_shapes=[
            weights,
            weights,
            weights,
            parts(lambda n: (4, 8, n * TILE), BF16),
            parts(lambda n: (HALVES, 4, 4, n, 16, TILE), BF16),
            pieces(lambda n: (HALVES, 4, 4, n, 16, TILE), BF16),
            pltpu.VMEM((COLS, 3, 32, 8, TILE), F32),
            pltpu.VMEM((HALVES, COLS, 8, 16, TILE), BF16),
            pltpu.VMEM((HALVES, COLS, 8, 16, TILE), BF16),
            pltpu.VMEM((HALVES, 3, COLS, 16, 16, BLK), BF16),
            pieces(lambda n: (HALVES, 2, 2, n, 16, TILE), BF16),
            pieces(lambda n: (HALVES, 2, 4, n, 16, TILE), BF16),
            pieces(lambda n: (HALVES, 4, n, 16, TILE), BF16),
            pieces(lambda n: (HALVES, 3, n, 16, TILE), BF16),
            pieces(lambda n: (HALVES, 4, n // 2, 8, TILE), F32),
            pieces(lambda n: (HALVES, 3, n // 2, 8, TILE), F32),
            pltpu.VMEM((3, 8, 128), jnp.int32),
            pltpu.VMEM((3, 8, 128), jnp.int32),
            pltpu.SMEM((3, 8, 128), jnp.int32),
            small, small, small, dma((1,)), dma((1,)), dma((1,)),
            dma((3, 3)), dma((3, 3)), three, three, dma((HALVES, 3, 2, 2)), dma((HALVES, 3, 2, 2)), two, two, cols, cols, cols, cols,
            out_two, out_two, out_two, out_two, out_three, out_three, out_three, out_three, out_two, out_two,
            *[pltpu.SMEM(a.shape, jnp.int32) for a in (gate_slots, up_slots, down_slots, block_counts)],
            dma((4,)), small,
        ],
        compiler_params=pltpu.CompilerParams(
            collective_id=0, has_side_effects=True, vmem_limit_bytes=60 * 2**20
        ),
    )(tokens, gate_blocks, gate_slots, up_blocks, up_slots, down_blocks, down_slots, block_counts)


def solution(mesh):
    return jax.shard_map(
        on_device,
        mesh=mesh,
        in_specs=(
            P(("seq", "tensor"), None),
            P("tensor", "seq", None, None),
            P("tensor", "seq"),
            P("tensor", "seq", None, None),
            P("tensor", "seq"),
            P("tensor", "seq", None, None),
            P("tensor", "seq"),
            P("tensor", None),
        ),
        out_specs=P(("seq", "tensor"), None),
        check_vma=False,
    )
```

```python
import jax
import jax.numpy as jnp
from jax import lax
from jax.experimental import pallas as pl
from jax.experimental.pallas import tpu as pltpu
from jax.sharding import PartitionSpec as P

MESH = pl.DeviceIdType.MESH
BF16, F32 = jnp.bfloat16, jnp.float32
BLK = 128
TILE = 256
COLS = 7
OWN = 84
NONE = 2 * OWN
TILES = (12, 8, 12)
FIRST = (0, TILES[0], TILES[0] + TILES[1])
AXES = (("y", "x", "z"), ("x", "z", "y"), ("z", "y", "x"))
PARTS = range(3)
HALVES = 2
PIECES = ((0, 0, 6), (1, 12, 4), (2, 20, 6), (0, 6, 6), (1, 16, 4), (2, 26, 6))
ALL = range(len(PIECES))


def swap4(a, b):
    low = lax.broadcasted_iota(jnp.int32, a.shape, 0) < 4
    return jnp.where(low, a, pltpu.roll(b, 4, 0)), jnp.where(low, pltpu.roll(a, 4, 0), b)


def kernel(
    tok, gate_in, gate_slots_in, up_in, up_slots_in, down_in, down_slots_in, counts_in, out,
    gate_w, up_w, down_w, first, xs, ys, acc, esend, erecv, hid, r0, r1, s2, r2, s3, r3, tab_v, tab_o, tab,
    w_sem, w_send, w_recv, t_send, t_recv, t_sem, a1s, a1r, a2s, a2r, a3s, a3r, a4s, a4r, es, er, hs, hr,
    b0s, b0r, b1s, b1r, b2s, b2r, b3s, b3r, b4s, b4r,
    gate_slots, up_slots, down_slots, counts, slot_sem, tok_sem,
):
    s, t = lax.axis_index("seq"), lax.axis_index("tensor")
    yl, core = lax.div(s, 2), lax.rem(s, 2)
    z, x, yh = lax.div(t, 8), lax.rem(lax.div(t, 2), 4), lax.rem(t, 2)
    here = {"z": z, "x": x, "y": yh * 2 + yl, "core": core}

    def device(**moved):
        c = {**here, **moved}
        return (lax.rem(c["y"], 2) * 2 + c["core"], c["z"] * 8 + c["x"] * 2 + lax.div(c["y"], 2))

    def at(axis, off):
        return lax.rem(here[axis] + off, 4)

    def along(axis, off):
        return device(**{axis: at(axis, off)})

    mate = device(core=1 - core)
    pair = device(y=yh * 2 + (1 - yl))
    started = {}

    def remote(src, dst, send, recv, dev):
        return pltpu.make_async_remote_copy(
            src_ref=src, dst_ref=dst, send_sem=send, recv_sem=recv, device_id=dev, device_id_type=MESH
        )

    def start(*args):
        c = remote(*args)
        c.start()
        started[id(c)] = c
        return c

    barrier = pltpu.get_barrier_semaphore()
    for dev in [mate] + [along(a, o) for a in "xyz" for o in (1, 2, 3)]:
        pl.semaphore_signal(barrier, inc=1, device_id=dev, device_id_type=MESH)
    loads = []
    for p in PARTS:
        cols = pl.ds(FIRST[p] * TILE, TILES[p] * TILE)
        loads.append(pltpu.make_async_copy(tok.at[:, cols], first[p].at[here[AXES[p][0]]], tok_sem.at[p]))
    slot_loads = [
        pltpu.make_async_copy(src, dst, slot_sem.at[i])
        for i, (src, dst) in enumerate(
            ((gate_slots_in, gate_slots), (up_slots_in, up_slots), (down_slots_in, down_slots), (counts_in, counts))
        )
    ]
    for c in loads + slot_loads:
        c.start()
    pl.semaphore_wait(barrier, 10)

    gather1, gather2, gather3, gather4 = {}, {}, {}, {}
    for p in PARTS:
        d1 = AXES[p][0]
        cols = pl.ds(FIRST[p] * TILE, TILES[p] * TILE)
        for o in (1, 2, 3):
            gather1[p, o] = start(
                tok.at[:, cols], first[p].at[here[d1]], a1s.at[p, o - 1], a1r.at[p, o - 1], along(d1, o)
            )
    weights = ((gate_in, gate_w), (up_in, up_w), (down_in, down_w))
    local, swap = [], []
    for m, (src, dst) in enumerate(weights):
        local.append(pltpu.make_async_copy(src.at[0], dst.at[pl.ds(0, OWN)], w_sem.at[m]))
        swap.append(remote(src.at[0], dst.at[pl.ds(OWN, OWN)], w_send.at[m], w_recv.at[m], mate))
        local[m].start()
        if m < 2:
            swap[m].start()
        dst[NONE] = jnp.zeros((BLK, BLK), BF16)

    places = lax.broadcasted_iota(jnp.int32, (8, 128), 0) * 128 + lax.broadcasted_iota(jnp.int32, (8, 128), 1)

    def tables():
        for m, slots in enumerate((gate_slots, up_slots, down_slots)):
            live = counts[0, m] - s * OWN

            def enter(j, table, m=m, slots=slots, live=live):
                i = slots[0, j]
                if m < 2:
                    place = lax.rem(i, COLS) * 128 + lax.div(i, COLS)
                else:
                    place = lax.div(i, 64) * 128 + lax.rem(i, 64)
                return jnp.where((places == place) & (j < live), j, table)

            tab_v[m] = lax.fori_loop(0, OWN, enter, jnp.full((8, 128), NONE, jnp.int32))

    def start_gather2(h, p):
        d1, d2, d3 = AXES[p]
        part = xs[p].at[h, here[d3], here[d2]]
        for o in (1, 2, 3):
            gather2[h, p, o] = start(part, part, a2s.at[h, p, o - 1], a2r.at[h, p, o - 1], along(d2, o))

    for p in PARTS:
        d1, d2, d3 = AXES[p]
        for o in (1, 2, 3):
            gather1[p, o].wait_recv()
        loads[p].wait()

        def regroup(n, _, p=p, d2=d2, d3=d3):
            cols = pl.ds(pl.multiple_of(n * TILE, TILE), TILE)
            rows = [first[p][q, :, cols].astype(F32) for q in range(4)]
            top, end = swap4(rows[0], rows[1]), swap4(rows[2], rows[3])
            for h in range(HALVES):
                xs[p][h, here[d3], here[d2], n] = jnp.concatenate([top[h], end[h]], 0).astype(BF16)
            return 0

        lax.fori_loop(0, TILES[p], regroup, 0)
        start_gather2(0, p)
    for p in PARTS:
        start_gather2(1, p)
    for c in slot_loads:
        c.wait()
    tables()
    swap_tab = remote(tab_v, tab_o, t_send.at[0], t_recv.at[0], mate)
    swap_tab.start()

    def start_gather3(h, p):
        d3 = AXES[p][2]
        for o in (1, 2, 3):
            gather2[h, p, o].wait_recv()
        for k in range(2):
            for i, o in enumerate((1, 3)):
                part = xs[p].at[h, here[d3], pl.ds(2 * (k if i == 0 else 1 - k), 2)]
                gather3[h, p, i, k] = start(part, part, a3s.at[h, p, i, k], a3r.at[h, p, i, k], along(d3, o))

    def start_gather4(h, p):
        d3 = AXES[p][2]
        for i, o in enumerate((1, 3)):
            gather3[h, p, i, 0].wait_recv()
            part = xs[p].at[h, at(d3, 4 - o), pl.ds(2 * i, 2)]
            gather4[h, p, i] = start(part, part, a4s.at[h, p, i], a4r.at[h, p, i], along(d3, o))

    for p in PARTS:
        start_gather3(0, p)
    for p in PARTS:
        start_gather4(0, p)
    for p in PARTS:
        start_gather3(1, p)

    swap_tab.wait()
    tab_v[...] = jnp.minimum(tab_v[...], tab_o[...] + OWN)
    to_scalar = pltpu.make_async_copy(tab_v, tab, t_sem.at[0])
    to_scalar.start()
    to_scalar.wait()
    for m in range(2):
        local[m].wait()
        swap[m].wait()

    def project(p, h, j):
        left = jnp.concatenate([xs[p][h, :, :, n].reshape(256, TILE) for n in range(TILES[p])], 1)
        rows = []
        for r in range(2 * FIRST[p], 2 * (FIRST[p] + TILES[p])):
            rows.append(jnp.concatenate([gate_w[tab[0, j, r]], up_w[tab[1, j, r]]], 1))
        acc[j, p] = jnp.dot(left, jnp.concatenate(rows, 0), preferred_element_type=F32).reshape(32, 8, TILE)

    def sums(j, kz, kx):
        tiles = {}
        for ky in range(2):
            v = {}
            for i in range(2):
                zz, xx = 2 * kz + i, 2 * kx + i
                y0, y1 = (acc[j, 1, ((2 * ky + k) * 4 + zz) * 2 + kx] for k in range(2))
                v[1, i, 0], v[1, i, 1] = swap4(y0, y1)
                y0, y1 = (acc[j, 2, (xx * 4 + 2 * ky + k) * 2 + kz] for k in range(2))
                v[2, 0, i], v[2, 1, i] = swap4(y0, y1)
            for i in range(2):
                for k in range(2):
                    own = acc[j, 0, ((2 * kz + i) * 4 + 2 * kx + k) * 2 + ky]
                    tiles[i, k, ky] = own + v[1, i, k] + v[2, i, k]
        return {(i, k): jnp.concatenate([tiles[i, k, 0], tiles[i, k, 1]], 0) for i in range(2) for k in range(2)}

    def exchange(h, j):
        return remote(esend.at[h, j], erecv.at[h, j], es.at[h, j], er.at[h, j], pair)

    def give(h, j):
        mine = hid.at[h, 0, j, pl.ds(yl * 8, 8)]
        return remote(mine, mine, hs.at[h, j], hr.at[h, j], pair)

    def project_all(h, lo, hi):
        def body(j, _):
            for p in PARTS:
                project(p, h, j)
            for kx in range(2):
                for (i, k), v in sums(j, 1 - yl, kx).items():
                    esend[h, j, i * 4 + 2 * kx + k] = v.astype(BF16)
            exchange(h, j).start()
            return 0

        lax.fori_loop(lo, hi, body, 0)

    def finish(h):
        def body(j, _):
            exchange(h, j).wait_recv()
            for kx in range(2):
                for (i, k), v in sums(j, yl, kx).items():
                    row = i * 4 + 2 * kx + k
                    v = v + erecv[h, j, row].astype(F32)
                    g, u = v[:, :BLK], v[:, BLK:]
                    hid[h, 0, j, yl * 8 + row] = (g / (1.0 + jnp.exp(-g)) * u).astype(BF16)
            give(h, j).start()
            return 0

        lax.fori_loop(0, COLS, body, 0)

    def reorder(h):
        def body(j, _):
            give(h, j).wait_recv()
            v = hid[h, 0, j].astype(F32)

            def group(zz, xx, ky):
                return v[zz * 4 + xx, 8 * ky : 8 * ky + 8]

            for ky in range(2):
                for i in range(4):
                    a = [swap4(group(i, 2 * k, ky), group(i, 2 * k + 1, ky)) for k in range(2)]
                    b = [swap4(group(2 * k, i, ky), group(2 * k + 1, i, ky)) for k in range(2)]
                    for k in range(2):
                        yy = 2 * ky + k
                        hid[h, 1, j, yy * 4 + i] = jnp.concatenate([a[0][k], a[1][k]], 0).astype(BF16)
                        hid[h, 2, j, i * 4 + yy] = jnp.concatenate([b[0][k], b[1][k]], 0).astype(BF16)
            return 0

        lax.fori_loop(0, COLS, body, 0)

    scatter0, scatter1, scatter2, scatter3, scatter4 = {}, {}, {}, {}, {}

    def down(h, q):
        p, a, tiles = PIECES[q]
        d3 = AXES[p][2]
        left = jnp.concatenate([hid[h, p, j].reshape(256, BLK) for j in range(COLS)], 1)
        for n in range(tiles):
            col = 2 * (a + n)
            rows = []
            for j in range(COLS):
                rows.append(jnp.concatenate([down_w[tab[2, j, col]], down_w[tab[2, j, col + 1]]], 1))
            v = jnp.dot(left, jnp.concatenate(rows, 0), preferred_element_type=F32)
            ys[q][h, :, :, n] = v.astype(BF16).reshape(4, 4, 16, TILE)
        for i, o in enumerate((1, 3)):
            src = ys[q].at[h, at(d3, 2), pl.ds(2 * i, 2)]
            scatter0[h, q, i] = start(src, r0[q].at[h, i], b0s.at[h, q, i], b0r.at[h, q, i], along(d3, o))
        for i, o in enumerate((1, 3)):
            ready = pl.ds(2 - 2 * i, 2)
            src = ys[q].at[h, at(d3, o), ready]
            scatter4[h, q, i] = start(src, r1[q].at[h, i, ready], b4s.at[h, q, i], b4r.at[h, q, i], along(d3, o))

    def pass_on(h, q):
        p, a, tiles = PIECES[q]
        d3 = AXES[p][2]
        for i, o in enumerate((1, 3)):
            scatter0[h, q, i].wait_recv()

            def body(n, _, i=i, o=o):
                for k in range(2):
                    v = ys[q][h, at(d3, o), 2 * i + k, n].astype(F32) + r0[q][h, i, k, n].astype(F32)
                    ys[q][h, at(d3, o), 2 * i + k, n] = v.astype(BF16)
                return 0

            lax.fori_loop(0, tiles, body, 0)
            rest = pl.ds(2 * i, 2)
            src = ys[q].at[h, at(d3, o), rest]
            scatter1[h, q, i] = start(src, r1[q].at[h, i, rest], b1s.at[h, q, i], b1r.at[h, q, i], along(d3, o))

    def sum1(h, q, k, n):
        v = ys[q][h, here[AXES[PIECES[q][0]][2]], k, n].astype(F32)
        return v + r1[q][h, 0, k, n].astype(F32) + r1[q][h, 1, k, n].astype(F32)

    def add1(h, q):
        p, a, tiles = PIECES[q]
        d2 = AXES[p][1]
        for i in range(2):
            scatter1[h, q, i].wait_recv()
            scatter4[h, q, i].wait_recv()

        def body(n, _):
            for k in range(4):
                s2[q][h, k, n] = sum1(h, q, k, n).astype(BF16)
            return 0

        lax.fori_loop(0, tiles, body, 0)
        for o in (1, 2, 3):
            src = s2[q].at[h, at(d2, o)]
            scatter2[h, q, o] = start(src, r2[q].at[h, o - 1], b2s.at[h, q, o - 1], b2r.at[h, q, o - 1], along(d2, o))

    def sum2(h, q, n):
        v = sum1(h, q, here[AXES[PIECES[q][0]][1]], n)
        for o in range(3):
            v = v + r2[q][h, o, n].astype(F32)
        return v

    def add2(h, q):
        p, a, tiles = PIECES[q]
        d1 = AXES[p][0]
        for o in (1, 2, 3):
            scatter2[h, q, o].wait_recv()

        def body(n, _):
            a, b = sum2(h, q, 2 * n), sum2(h, q, 2 * n + 1)
            for k in range(2):
                u, v = swap4(a[8 * k : 8 * k + 8], b[8 * k : 8 * k + 8])
                s3[q][h, 2 * k, n] = u
                s3[q][h, 2 * k + 1, n] = v
            return 0

        lax.fori_loop(0, tiles // 2, body, 0)
        for o in (1, 2, 3):
            src = s3[q].at[h, at(d1, o)]
            scatter3[h, q, o] = start(src, r3[q].at[h, o - 1], b3s.at[h, q, o - 1], b3r.at[h, q, o - 1], along(d1, o))

    def add3(q):
        p, a, tiles = PIECES[q]
        d1 = AXES[p][0]
        for h in range(HALVES):
            for o in (1, 2, 3):
                scatter3[h, q, o].wait_recv()

        def body(n, _):
            v = [s3[q][h, here[d1], n] + r3[q][h, 0, n] + r3[q][h, 1, n] + r3[q][h, 2, n] for h in range(HALVES)]
            for k, rows in enumerate(swap4(*v)):
                out[:, pl.ds(pl.multiple_of((a + 2 * n + k) * TILE, TILE), TILE)] = rows.astype(BF16)
            return 0

        lax.fori_loop(0, tiles // 2, body, 0)

    def end_gather4(h):
        for p in PARTS:
            for i in range(2):
                gather3[h, p, i, 1].wait_recv()
                gather4[h, p, i].wait_recv()

    def each(step, *args):
        for q in ALL:
            step(*args, q)

    end_gather4(0)
    project_all(0, 0, 2)
    for p in PARTS:
        start_gather4(1, p)
    project_all(0, 2, COLS)
    swap[2].start()
    finish(0)
    end_gather4(1)
    project_all(1, 0, COLS)
    reorder(0)
    local[2].wait()
    swap[2].wait()
    each(down, 0)
    finish(1)
    each(pass_on, 0)
    reorder(1)
    each(down, 1)
    each(pass_on, 1)
    each(add1, 0)
    each(add1, 1)
    each(add2, 0)
    each(add2, 1)
    each(add3)

    def sent(j, _):
        for h in range(HALVES):
            exchange(h, j).wait_send()
            give(h, j).wait_send()
        return 0

    lax.fori_loop(0, COLS, sent, 0)
    for c in started.values():
        c.wait_send()


def on_device(tokens, gate_blocks, gate_slots, up_blocks, up_slots, down_blocks, down_slots, block_counts):
    vmem = pl.BlockSpec(memory_space=pltpu.VMEM)
    hbm = pl.BlockSpec(memory_space=pl.ANY)
    dma = pltpu.SemaphoreType.DMA

    def parts(shape, dtype):
        return [pltpu.VMEM(shape(n), dtype) for n in TILES]

    def pieces(shape, dtype):
        return [pltpu.VMEM(shape(n), dtype) for _, _, n in PIECES]

    weights = pltpu.VMEM((NONE + 1, BLK, BLK), BF16)
    small, three, two, cols = dma((3,)), dma((HALVES, 3, 3)), dma((HALVES, 3, 2)), dma((HALVES, COLS))
    many = len(PIECES)
    out_two, out_three = dma((HALVES, many, 2)), dma((HALVES, many, 3))
    return pl.pallas_call(
        kernel,
        name="layer",
        out_shape=jax.ShapeDtypeStruct(tokens.shape, BF16),
        in_specs=[hbm] * 8,
        out_specs=vmem,
        scratch_shapes=[
            weights,
            weights,
            weights,
            parts(lambda n: (4, 8, n * TILE), BF16),
            parts(lambda n: (HALVES, 4, 4, n, 16, TILE), BF16),
            pieces(lambda n: (HALVES, 4, 4, n, 16, TILE), BF16),
            pltpu.VMEM((COLS, 3, 32, 8, TILE), F32),
            pltpu.VMEM((HALVES, COLS, 8, 16, TILE), BF16),
            pltpu.VMEM((HALVES, COLS, 8, 16, TILE), BF16),
            pltpu.VMEM((HALVES, 3, COLS, 16, 16, BLK), BF16),
            pieces(lambda n: (HALVES, 2, 2, n, 16, TILE), BF16),
            pieces(lambda n: (HALVES, 2, 4, n, 16, TILE), BF16),
            pieces(lambda n: (HALVES, 4, n, 16, TILE), BF16),
            pieces(lambda n: (HALVES, 3, n, 16, TILE), BF16),
            pieces(lambda n: (HALVES, 4, n // 2, 8, TILE), F32),
            pieces(lambda n: (HALVES, 3, n // 2, 8, TILE), F32),
            pltpu.VMEM((3, 8, 128), jnp.int32),
            pltpu.VMEM((3, 8, 128), jnp.int32),
            pltpu.SMEM((3, 8, 128), jnp.int32),
            small, small, small, dma((1,)), dma((1,)), dma((1,)),
            dma((3, 3)), dma((3, 3)), three, three, dma((HALVES, 3, 2, 2)), dma((HALVES, 3, 2, 2)), two, two, cols, cols, cols, cols,
            out_two, out_two, out_two, out_two, out_three, out_three, out_three, out_three, out_two, out_two,
            *[pltpu.SMEM(a.shape, jnp.int32) for a in (gate_slots, up_slots, down_slots, block_counts)],
            dma((4,)), small,
        ],
        compiler_params=pltpu.CompilerParams(
            collective_id=0, has_side_effects=True, vmem_limit_bytes=60 * 2**20
        ),
    )(tokens, gate_blocks, gate_slots, up_blocks, up_slots, down_blocks, down_slots, block_counts)


def solution(mesh):
    return jax.shard_map(
        on_device,
        mesh=mesh,
        in_specs=(
            P(("seq", "tensor"), None),
            P("tensor", "seq", None, None),
            P("tensor", "seq"),
            P("tensor", "seq", None, None),
            P("tensor", "seq"),
            P("tensor", "seq", None, None),
            P("tensor", "seq"),
            P("tensor", None),
        ),
        out_specs=P(("seq", "tensor"), None),
        check_vma=False,
    )
```
